256 devices in a mesh: section: 16 (over y, x), expert: 16 (over z, core).
Axes of the slice: x: 4, y: 4, z: 8, core: 2. Of those that a mesh axis runs over, the one named last changes fastest.
Arguments:
- layer_input: bfloat16 [16, 1024, 4096], P('section', 'expert'), may hold values from -6 to 6
- cotangent: bfloat16 [16, 1024, 4096], P('section', 'expert'), may hold values from -6 to 6
- gate_weight: bfloat16 [16, 4096, 6144], P('section', None, 'expert'), may hold values from -0.09375 to 0.09375
- up_weight: bfloat16 [16, 4096, 6144], P('section', None, 'expert'), may hold values from -0.09375 to 0.09375
- down_weight: bfloat16 [16, 6144, 4096], P('section', 'expert'), may hold values from -0.15625 to 0.15625
- stashed_pre: bfloat16 [16, 16, 24, 2, 6144], P('section', None, None, None, 'expert'), may hold values from -6 to 6
- first_ids: int32 [16, 1024, 1], P('section', 'expert'), may hold values from 0 to 3; in each aligned block of 64 rows (0 to 63, 64 to 127, ..., all dimensions but the last counted through in order) at most 24 rows name the same one
- first_gates: float32 [16, 1024, 1], P('section', 'expert'), may hold values from 0.3 to 1
- second_ids: int32 [16, 1024, 1], P('section', 'expert'), may hold values from 0 to 3; in each aligned block of 64 rows (0 to 63, 64 to 127, ..., all dimensions but the last counted through in order) at most 24 rows name the same one
- second_gates: float32 [16, 1024, 1], P('section', 'expert'), may hold values from 0.3 to 1
- keep_mask: int32 [16, 1024], P('section', 'expert'), may hold values 0 or 1
Outputs:
- next_input: bfloat16 [16, 1024, 4096], P('section', 'expert')
- prev_cotangent: bfloat16 [16, 1024, 4096], P('section', 'expert')
The draws below stay inside these ranges and needn't reach their ends.
Inputs may be any that keep to these rules, and one draw needn't show every extreme that they name: `first_ids`: in each aligned block of 64 rows (the rows of one device) the picks of a row are distinct and no expert is named more than 24 times; in some blocks one expert is named exactly 24 times. `second_ids`: as for first_ids.
All inputs are finite; a program needn't handle non-finite values. No bound on the sum of `keep_mask` on one device may be relied on, other than what follows from the above.
Results may differ from the reference program's by a relative error of at most 0.0048.
Values may be sent and summed in bfloat16 or wider, within the bound.
No kernel may reach another device: no remote copies, remote signals or barrier semaphores. Data moves between devices by JAX's collectives and lax.ppermute only.
A program may use at most 128 MiB of HBM per device.

```python
import math
import jax
import jax.numpy as jnp
import numpy as np
from jax import lax

D = 4096
HID = 1536
SHARDS = 4
TOPK = 1
TOK_DEV = 64
H_DEV = 384
EXPERTS = 4
CAP = 24
TOKENS = 1024
N_SECTION = 16
N_EXPERT = 16


def touch_ends(drawn, key, low, top_value):
    spot = [jax.random.randint(jax.random.fold_in(key, axis), (), 0, length) for axis, length in enumerate(drawn.shape)]
    widest = drawn.shape.index(max(drawn.shape))
    neighbour = spot[:widest] + [(spot[widest] + 1) % drawn.shape[widest]] + spot[widest + 1:]
    return drawn.at[tuple(spot)].set(low).at[tuple(neighbour)].set(top_value)


def block_scale(rng, shape, pieces, least, largest):
    loudness = 1.0
    for dim, blocks in pieces:
        steps = jax.random.uniform(jax.random.fold_in(jax.random.fold_in(rng, 6), dim), (blocks,), jnp.float32, least / len(pieces), largest / len(pieces))
        loudness = loudness * jnp.repeat(jnp.exp(steps), shape[dim] // blocks).reshape((-1,) + (1,) * (len(shape) - 1 - dim))
    return loudness


def routed_block(stream_key, own, number, rows, count, top, limit, skew):
    sequence = jax.random.permutation(stream_key, count)
    crowded, usual = portions_of(count, rows * top, limit, skew, True), portions_of(count, rows * top, limit, skew, False)
    places = jnp.arange(count)

    def named(tallies, offset_by):
        used = int((tallies > 0).sum())
        fixed = max(1, used // 4)
        shifted = fixed + (places - fixed + offset_by * (used - fixed)) % max(1, count - fixed)
        return jnp.zeros((count,), jnp.int32).at[sequence[jnp.where(places < fixed, places, shifted)]].set(jnp.asarray(tallies, jnp.int32))

    tallies = jnp.where(number % 4 == 0, named(crowded, number // 4), named(usual, number - number // 4 - 1))
    mixed = jax.random.permutation(jax.random.fold_in(own, 3), count)
    source_of, sink = mixed[0:count // 2 * 2:2], mixed[1:count // 2 * 2:2]
    margin = jnp.minimum(tallies[source_of] - 1, limit - tallies[sink]) // 2
    margin = jnp.where((source_of == sequence[0]) | (sink == sequence[0]) | (tallies[sink] == 0), 0, jnp.maximum(margin, 0))
    shifted = jax.random.randint(jax.random.fold_in(own, 4), (count // 2,), 0, 1 << 20) % (margin + 1)
    tallies = tallies.at[source_of].add(-shifted).at[sink].add(shifted)
    members = jnp.searchsorted(jnp.cumsum(tallies), jnp.arange(rows * top), side="right").astype(jnp.int32)
    grid = members.reshape(top, rows).T
    grid = grid[jax.random.permutation(jax.random.fold_in(own, 1), rows)]
    offset_by = jax.random.randint(jax.random.fold_in(own, 2), (rows, 1), 0, top)
    return jnp.take_along_axis(grid, (jnp.arange(top)[None, :] + offset_by) % top, axis=1)


def portions_of(count, total, most, lean, full):
    portions = [(1 << 20) // math.isqrt(grade ** lean) + 1 for grade in range(1, count + 1)]
    largest = most if full else min(most, max(-(-total // count), total * portions[0] // sum(portions)))
    least = 1 if total - largest >= count - 1 else 0
    counts, surplus = [largest] + [least] * (count - 1), total - largest - least * (count - 1)
    while surplus > 0:
        candidates = [i for i in range(1, count) if counts[i] < largest] or [i for i in range(1, count) if counts[i] < most]
        mass, left = sum([portions[i] for i in candidates]), surplus
        for i in candidates:
            addition = min(most - counts[i], max(1, left * portions[i] // mass), surplus)
            counts[i] = counts[i] + addition
            surplus = surplus - addition
    return np.array(counts)


def gaussian(own_key, dims, width, bound, shards=(), kind=jnp.bfloat16):
    drawn = jax.random.normal(own_key, dims, jnp.float32) * width
    if len(shards) > 0:
        drawn = block_scale(own_key, dims, shards, -0.22, 0.18) * drawn
    return jnp.clip(drawn, min=-bound, max=bound).astype(kind)


def setup_inputs(seed: int = 0) -> dict:
    arg_keys = jax.random.split(jax.random.key(seed), 12)
    layer_input = gaussian(arg_keys[0], (N_SECTION, TOKENS, D), 1.0, 6.0, ((0, 16), (1, 16)))
    cotangent = gaussian(arg_keys[1], (N_SECTION, TOKENS, D), 1.0, 6.0, ((0, 16), (1, 16)))
    gate_weight = gaussian(arg_keys[2], (N_SECTION, D, EXPERTS * HID), D ** -0.5, 0.09375, ((0, 16), (2, 16)))
    up_weight = gaussian(arg_keys[3], (N_SECTION, D, EXPERTS * HID), D ** -0.5, 0.09375, ((0, 16), (2, 16)))
    down_weight = gaussian(arg_keys[4], (N_SECTION, EXPERTS * HID, D), HID ** -0.5, 0.15625, ((0, 16), (1, 16)))
    stashed_pre = gaussian(arg_keys[5], (N_SECTION, N_EXPERT, CAP, 2, EXPERTS * HID), 1.0, 6.0, ((0, 16), (4, 16)))
    first_ids_keys = jax.random.split(jax.random.fold_in(arg_keys[6], 1), N_SECTION * TOKENS // TOK_DEV)
    first_ids_turns = jax.random.permutation(jax.random.fold_in(arg_keys[6], 3), N_SECTION * TOKENS // TOK_DEV)
    first_ids = jax.vmap(lambda own, number: routed_block(jax.random.fold_in(arg_keys[6], 2), own, number, TOK_DEV, EXPERTS, TOPK, CAP, 2))(first_ids_keys, first_ids_turns).reshape((N_SECTION, TOKENS, TOPK))
    first_gates = jnp.clip(0.3 + 0.7 * jax.random.uniform(arg_keys[7], (N_SECTION, TOKENS, TOPK), jnp.float32) ** block_scale(arg_keys[7], (N_SECTION, TOKENS, TOPK), ((0, 16), (1, 16)), -0.2, 0.2), 0.3, 1.0)
    second_ids_keys = jax.random.split(jax.random.fold_in(arg_keys[8], 1), N_SECTION * TOKENS // TOK_DEV)
    second_ids_turns = jax.random.permutation(jax.random.fold_in(arg_keys[8], 3), N_SECTION * TOKENS // TOK_DEV)
    second_ids = jax.vmap(lambda own, number: routed_block(jax.random.fold_in(arg_keys[8], 2), own, number, TOK_DEV, EXPERTS, TOPK, CAP, 2))(second_ids_keys, second_ids_turns).reshape((N_SECTION, TOKENS, TOPK))
    second_gates = jnp.clip(0.3 + 0.7 * jax.random.uniform(arg_keys[9], (N_SECTION, TOKENS, TOPK), jnp.float32) ** block_scale(arg_keys[9], (N_SECTION, TOKENS, TOPK), ((0, 16), (1, 16)), -0.2, 0.2), 0.3, 1.0)
    keep_mask = touch_ends((jax.random.randint(arg_keys[10], (N_SECTION, TOKENS), 0, 4) < 3).astype(jnp.int32), jax.random.fold_in(arg_keys[10], 1), 0, 1)
    return {"layer_input": layer_input, "cotangent": cotangent, "gate_weight": gate_weight, "up_weight": up_weight, "down_weight": down_weight, "stashed_pre": stashed_pre, "first_ids": first_ids, "first_gates": first_gates, "second_ids": second_ids, "second_gates": second_gates, "keep_mask": keep_mask}


def positions(route_ids, expert_count, capacity):
    flat_ids = route_ids.reshape(-1).astype(jnp.int32)
    onehot = (flat_ids[:, None] == jnp.arange(expert_count, dtype=jnp.int32)[None, :]).astype(jnp.int32)
    earlier = jnp.cumsum(onehot, axis=0) - onehot
    slot_count = jnp.sum(earlier * onehot, axis=1).astype(jnp.int32)
    return (flat_ids * capacity + slot_count).reshape(route_ids.shape).astype(jnp.int32)


def placement(slot_at, slot_total):
    match_table = jnp.arange(slot_total, dtype=jnp.int32)[:, None, None] == slot_at[None, :, :]
    return jnp.any(match_table, axis=2).astype(jnp.bfloat16)


def expert_forward(routed, gate_cols, up_cols, down_rows):
    gate_pre = jnp.dot(routed, gate_cols, preferred_element_type=jnp.float32)
    up_pre = jnp.dot(routed, up_cols, preferred_element_type=jnp.float32)
    hidden = (jax.nn.silu(gate_pre) * up_pre).astype(jnp.bfloat16)
    return jnp.dot(hidden, down_rows, preferred_element_type=jnp.float32).astype(jnp.bfloat16)


def expert_backward(routed, stash_rows, gate_cols, up_cols, down_rows):
    hidden_grad = jnp.dot(routed, down_rows.T, preferred_element_type=jnp.float32)
    gate_pre = stash_rows[:, 0, :].astype(jnp.float32)
    up_pre = stash_rows[:, 1, :].astype(jnp.float32)
    sigmoid_gate = jax.nn.sigmoid(gate_pre)
    grad_gate = (hidden_grad * up_pre * sigmoid_gate * (1.0 + gate_pre * (1.0 - sigmoid_gate))).astype(jnp.bfloat16)
    grad_up = (hidden_grad * gate_pre * sigmoid_gate).astype(jnp.bfloat16)
    input_grad = jnp.dot(grad_gate, gate_cols.T, preferred_element_type=jnp.float32)
    input_grad = input_grad + jnp.dot(grad_up, up_cols.T, preferred_element_type=jnp.float32)
    return input_grad.astype(jnp.bfloat16)


def one_section(section_args):
    tokens, grads, gate_weight, up_weight, down_weight, stashed, first_ids, first_gates, second_ids, second_gates, keep = section_args
    blocks = tokens.reshape(N_EXPERT, TOK_DEV, D)
    kept_grads = (grads * keep[:, None].astype(jnp.bfloat16)).reshape(N_EXPERT, TOK_DEV, D)
    first_at = jax.vmap(lambda block_ids: positions(block_ids, EXPERTS, CAP))(first_ids.reshape(N_EXPERT, TOK_DEV, TOPK))
    second_at = jax.vmap(lambda block_ids: positions(block_ids, EXPERTS, CAP))(second_ids.reshape(N_EXPERT, TOK_DEV, TOPK))
    first_place = jax.vmap(lambda slot_at: placement(slot_at, EXPERTS * CAP))(first_at)
    second_place = jax.vmap(lambda slot_at: placement(slot_at, EXPERTS * CAP))(second_at)
    first_rows = jnp.einsum('nrt,ntd->nrd', first_place.astype(jnp.float32), blocks.astype(jnp.float32)).astype(jnp.bfloat16)
    second_rows = jnp.einsum('nrt,ntd->nrd', second_place.astype(jnp.float32), kept_grads.astype(jnp.float32)).astype(jnp.bfloat16)

    def per_expert(expert):
        routed_first = lax.dynamic_slice_in_dim(first_rows, expert * CAP, CAP, 1).reshape(N_EXPERT * CAP, D)
        routed_second = lax.dynamic_slice_in_dim(second_rows, expert * CAP, CAP, 1).reshape(N_EXPERT * CAP, D)
        total_first = jnp.zeros((N_EXPERT * CAP, D), jnp.float32)
        total_second = jnp.zeros((N_EXPERT * CAP, D), jnp.float32)
        for quarter in range(SHARDS):
            offset = ((expert * SHARDS + quarter) * H_DEV).astype(jnp.int32)
            gate_cols = lax.dynamic_slice_in_dim(gate_weight, offset, H_DEV, 1)
            up_cols = lax.dynamic_slice_in_dim(up_weight, offset, H_DEV, 1)
            down_rows = lax.dynamic_slice_in_dim(down_weight, offset, H_DEV, 0)
            stash_rows = lax.dynamic_slice_in_dim(stashed, offset, H_DEV, 3).reshape(N_EXPERT * CAP, 2, H_DEV)
            total_first = total_first + expert_forward(routed_first, gate_cols, up_cols, down_rows).astype(jnp.float32)
            total_second = total_second + expert_backward(routed_second, stash_rows, gate_cols, up_cols, down_rows).astype(jnp.float32)
        return total_first.astype(jnp.bfloat16).reshape(N_EXPERT, CAP, D), total_second.astype(jnp.bfloat16).reshape(N_EXPERT, CAP, D)

    first_sums, second_sums = lax.map(per_expert, jnp.arange(EXPERTS, dtype=jnp.int32))
    first_sums = jnp.transpose(first_sums, (1, 0, 2, 3)).reshape(N_EXPERT, EXPERTS * CAP, D)
    second_sums = jnp.transpose(second_sums, (1, 0, 2, 3)).reshape(N_EXPERT, EXPERTS * CAP, D)
    first_picked = jax.vmap(lambda summed, slot_at: jnp.take(summed, slot_at, axis=0))(first_sums, first_at).astype(jnp.float32)
    second_picked = jax.vmap(lambda summed, slot_at: jnp.take(summed, slot_at, axis=0))(second_sums, second_at).astype(jnp.float32)
    first_branch = jnp.sum(first_picked * first_gates.reshape(N_EXPERT, TOK_DEV, TOPK)[..., None], axis=2)
    second_branch = jnp.sum(second_picked * second_gates.reshape(N_EXPERT, TOK_DEV, TOPK)[..., None], axis=2)
    mixed_out = (blocks.astype(jnp.float32) + first_branch).astype(jnp.bfloat16).reshape(TOKENS, D)
    keep_float = keep.reshape(N_EXPERT, TOK_DEV)[..., None].astype(jnp.float32)
    grad_out = (keep_float * (grads.reshape(N_EXPERT, TOK_DEV, D).astype(jnp.float32) + second_branch)).astype(jnp.bfloat16).reshape(TOKENS, D)
    return mixed_out, grad_out


def reference(layer_input, cotangent, gate_weight, up_weight, down_weight, stashed_pre, first_ids, first_gates, second_ids, second_gates, keep_mask):
    mixed_all, grad_all = lax.map(one_section, (layer_input, cotangent, gate_weight, up_weight, down_weight, stashed_pre, first_ids, first_gates, second_ids, second_gates, keep_mask))
    return jnp.roll(mixed_all, 1, axis=0), jnp.roll(grad_all, -1, axis=0)
```

```python
import jax
import jax.numpy as jnp
from jax import lax
from jax.sharding import PartitionSpec as P

REACH = 4


def routes(devices):
    chips = devices // 2

    def near(step, back):
        route = []
        for chip in range(chips):
            origin = (chip + (step if chip % 2 else -step)) % chips
            for core in range(2):
                pair = (2 * origin + core, 2 * chip + core)
                route.append(pair[::-1] if back else pair)
        return route

    across = [(i, i ^ 2) for i in range(devices)]
    beside = [(i, i ^ 1) for i in range(devices)]
    return near, across, beside


def message_of(ids, chip, pairs):
    ahead = (ids - chip // 2) % pairs
    even = jnp.where(ahead == 3, 1, jnp.where(ahead == 1, 2, jnp.where(ahead == 2, 3, 0)))
    odd = jnp.where(ahead == 1, 1, jnp.where(ahead == 3, 2, jnp.where(ahead == 2, 3, 0)))
    return jnp.where(chip % 2 == 0, even, odd)


def places(route_ids, chip, pairs, capacity):
    ids = route_ids.reshape(-1)
    count = ids.shape[0]
    row = lax.broadcasted_iota(jnp.int32, (count, count), 0)
    column = lax.broadcasted_iota(jnp.int32, (count, count), 1)
    earlier = (ids[:, None] == ids[None, :]) & (row < column)
    slot = jnp.sum(earlier.astype(jnp.int32), axis=0)
    return message_of(ids, chip, pairs) * capacity + slot


def placement(slot_at, slot_total):
    rows = lax.broadcasted_iota(jnp.int32, (slot_total, slot_at.shape[0]), 0)
    return (rows == slot_at[None, :]).astype(jnp.bfloat16)


def expert_forward(routed, gate_cols, up_cols, down_rows):
    gate_pre = jnp.dot(routed, gate_cols, preferred_element_type=jnp.float32)
    up_pre = jnp.dot(routed, up_cols, preferred_element_type=jnp.float32)
    hidden = (jax.nn.silu(gate_pre) * up_pre).astype(jnp.bfloat16)
    return jnp.dot(hidden, down_rows, preferred_element_type=jnp.float32).astype(jnp.bfloat16)


def expert_backward(routed, stash_rows, gate_cols, up_cols, down_rows):
    hidden_grad = jnp.dot(routed, down_rows.T, preferred_element_type=jnp.float32)
    gate_pre = stash_rows[:, 0, :].astype(jnp.float32)
    up_pre = stash_rows[:, 1, :].astype(jnp.float32)
    sigmoid_gate = jax.nn.sigmoid(gate_pre)
    grad_gate = (
        hidden_grad * up_pre * sigmoid_gate * (1.0 + gate_pre * (1.0 - sigmoid_gate))
    ).astype(jnp.bfloat16)
    grad_up = (hidden_grad * gate_pre * sigmoid_gate).astype(jnp.bfloat16)
    input_grad = jnp.dot(grad_gate, gate_cols.T, preferred_element_type=jnp.float32)
    input_grad = input_grad + jnp.dot(grad_up, up_cols.T, preferred_element_type=jnp.float32)
    return input_grad.astype(jnp.bfloat16)


def dispatch(rows, capacity, near, across, beside):
    parts = [rows[:capacity]] + [
        lax.ppermute(rows[k * capacity : (k + 1) * capacity], "expert", near(k, False))
        for k in range(1, REACH)
    ]
    close = jnp.concatenate(parts, axis=0)
    distant = lax.ppermute(close, "expert", across)
    half = jnp.concatenate([close, distant], axis=0)
    return jnp.concatenate([half, lax.ppermute(half, "expert", beside)], axis=0)


def collect(made, capacity, near, across, beside):
    half_rows = made.shape[0] // 2
    near_rows = half_rows // 2
    half = made[:half_rows].astype(jnp.float32) + lax.ppermute(
        made[half_rows:], "expert", beside
    ).astype(jnp.float32)
    distant = lax.ppermute(half[near_rows:].astype(jnp.bfloat16), "expert", across)
    close = (half[:near_rows] + distant.astype(jnp.float32)).astype(jnp.bfloat16)
    parts = [close[:capacity]] + [
        lax.ppermute(close[k * capacity : (k + 1) * capacity], "expert", near(k, True))
        for k in range(1, REACH)
    ]
    return jnp.concatenate(parts, axis=0)


def combine(placed, back, gate_values):
    picked = lax.dot_general(
        placed, back, (((0,), (0,)), ((), ())), preferred_element_type=jnp.float32
    )
    return picked * gate_values


def local(
    layer_input,
    cotangent,
    gate_weight,
    up_weight,
    down_weight,
    stashed_pre,
    first_ids,
    first_gates,
    second_ids,
    second_gates,
    keep_mask,
):
    devices = lax.axis_size("expert")
    sections = lax.axis_size("section")
    chips = devices // 2
    pairs = chips // 2
    capacity = stashed_pre.shape[2]
    slots = pairs * capacity
    hidden_local = gate_weight.shape[2]
    near, across, beside = routes(devices)
    me = lax.axis_index("expert")
    chip, core = me // 2, me % 2
    tokens_in = layer_input[0]
    keep_rows = keep_mask[0]
    kept_grads = cotangent[0] * keep_rows[:, None].astype(jnp.bfloat16)
    first_placed = placement(places(first_ids[0], chip, pairs, capacity), slots)
    second_placed = placement(places(second_ids[0], chip, pairs, capacity), slots)
    first_rows = jnp.dot(first_placed, tokens_in, preferred_element_type=jnp.float32).astype(
        jnp.bfloat16
    )
    second_rows = jnp.dot(second_placed, kept_grads, preferred_element_type=jnp.float32).astype(
        jnp.bfloat16
    )
    order = []
    for which in (core, 1 - core):
        for here in (chip, chip ^ 1):
            for step in range(REACH):
                origin = (here + jnp.where(here % 2 == 0, -step, step)) % chips
                order.append(2 * origin + which)
    stash_local = jnp.concatenate(
        [lax.dynamic_index_in_dim(stashed_pre[0], block, 0, False) for block in order]
    )
    gate_cols = gate_weight[0]
    up_cols = up_weight[0]
    down_rows = down_weight[0]

    held_second = dispatch(second_rows, capacity, near, across, beside)
    held_first = dispatch(first_rows, capacity, near, across, beside)
    made_second = expert_backward(held_second, stash_local, gate_cols, up_cols, down_rows)
    made_first = expert_forward(held_first, gate_cols, up_cols, down_rows)
    back_second = collect(made_second, capacity, near, across, beside)
    back_first = collect(made_first, capacity, near, across, beside)
    first_branch = combine(first_placed, back_first, first_gates[0])
    second_branch = combine(second_placed, back_second, second_gates[0])
    mixed_out = (tokens_in.astype(jnp.float32) + first_branch).astype(jnp.bfloat16)
    keep_float = keep_rows[:, None].astype(jnp.float32)
    grad_out = (keep_float * (cotangent[0].astype(jnp.float32) + second_branch)).astype(
        jnp.bfloat16
    )
    onward = [(i, (i + 1) % sections) for i in range(sections)]
    backward = [((i + 1) % sections, i) for i in range(sections)]
    moved_back = lax.ppermute(grad_out[None], "section", backward)
    moved_on = lax.ppermute(mixed_out[None], "section", onward)
    return (moved_on, moved_back)


def solution(mesh):
    placed = (
        P("section", "expert", None),
        P("section", "expert", None),
        P("section", None, "expert"),
        P("section", None, "expert"),
        P("section", "expert", None),
        P("section", None, None, None, "expert"),
        P("section", "expert", None),
        P("section", "expert", None),
        P("section", "expert", None),
        P("section", "expert", None),
        P("section", "expert"),
    )
    return jax.shard_map(
        local,
        mesh=mesh,
        in_specs=placed,
        out_specs=(P("section", "expert", None), P("section", "expert", None)),
        check_vma=False,
    )
```

```python
import jax
import jax.numpy as jnp
from jax import lax
from jax.sharding import PartitionSpec as P

REACH = 4


def routes(devices, sections):
    chips = devices // 2

    def nearer(step):
        for chip in range(chips):
            origin = (chip + (step if chip % 2 else -step)) % chips
            for core in range(2):
                yield 2 * origin + core, 2 * chip + core

    def out(step):
        return list(nearer(step))

    def home(step, onward):
        return [
            (s * devices + there, (s + onward) % sections * devices + origin)
            for s in range(sections)
            for origin, there in nearer(step)
        ]

    across = [(i, i ^ 2) for i in range(devices)]
    beside = [(i, i ^ 1) for i in range(devices)]
    return out, home, across, beside


def message_of(ids, chip, pairs):
    ahead = (ids - chip // 2) % pairs
    even = jnp.where(ahead == 3, 1, jnp.where(ahead == 1, 2, jnp.where(ahead == 2, 3, 0)))
    odd = jnp.where(ahead == 1, 1, jnp.where(ahead == 3, 2, jnp.where(ahead == 2, 3, 0)))
    return jnp.where(chip % 2 == 0, even, odd)


def places(route_ids, chip, pairs, capacity):
    ids = route_ids.reshape(-1)
    count = ids.shape[0]
    row = lax.broadcasted_iota(jnp.int32, (count, count), 0)
    column = lax.broadcasted_iota(jnp.int32, (count, count), 1)
    earlier = (ids[:, None] == ids[None, :]) & (row < column)
    slot = jnp.sum(earlier.astype(jnp.int32), axis=0)
    return message_of(ids, chip, pairs) * capacity + slot


def placement(slot_at, slot_total):
    rows = lax.broadcasted_iota(jnp.int32, (slot_total, slot_at.shape[0]), 0)
    return (rows == slot_at[None, :]).astype(jnp.bfloat16)


def after(value, *others):
    return lax.optimization_barrier((value, *others))[0]


def hidden_forward(routed, gate_cols, up_cols):
    gate_pre = jnp.dot(routed, gate_cols, preferred_element_type=jnp.float32)
    up_pre = jnp.dot(routed, up_cols, preferred_element_type=jnp.float32)
    return ((jax.nn.silu(gate_pre) * up_pre).astype(jnp.bfloat16),)


def made_forward(hidden, down_rows):
    return jnp.dot(hidden[0], down_rows, preferred_element_type=jnp.float32).astype(jnp.bfloat16)


def hidden_backward(routed, stash_rows, down_rows):
    hidden_grad = jnp.dot(routed, down_rows.T, preferred_element_type=jnp.float32)
    gate_pre = stash_rows[:, 0, :].astype(jnp.float32)
    up_pre = stash_rows[:, 1, :].astype(jnp.float32)
    sigmoid_gate = jax.nn.sigmoid(gate_pre)
    grad_gate = (
        hidden_grad * up_pre * sigmoid_gate * (1.0 + gate_pre * (1.0 - sigmoid_gate))
    ).astype(jnp.bfloat16)
    grad_up = (hidden_grad * gate_pre * sigmoid_gate).astype(jnp.bfloat16)
    return grad_gate, grad_up


def made_backward(hidden, gate_cols, up_cols):
    total = jnp.dot(hidden[0], gate_cols.T, preferred_element_type=jnp.float32)
    total = total + jnp.dot(hidden[1], up_cols.T, preferred_element_type=jnp.float32)
    return total.astype(jnp.bfloat16)


def dispatch(placed, rows, capacity, out, across):
    def picked(k):
        part = placed[k * capacity : (k + 1) * capacity]
        return jnp.dot(part, rows, preferred_element_type=jnp.float32).astype(jnp.bfloat16)

    own = picked(0)
    own_distant = lax.ppermute(own, "expert", across)
    near = jnp.concatenate(
        [lax.ppermute(picked(k), "expert", out(k)) for k in range(1, REACH)], axis=0
    )
    distant = lax.ppermute(near, "expert", across)
    return jnp.concatenate([own, own_distant, near, distant], axis=0)


def collect(mine, given, capacity, onward, sections, home, across, beside):
    came = lax.ppermute(given, "expert", beside)
    summed = mine.astype(jnp.float32) + came.astype(jnp.float32)
    own_near, own_far = summed[:capacity], summed[capacity : 2 * capacity]
    width = (REACH - 1) * capacity
    near, far = summed[2 * capacity : 2 * capacity + width], summed[2 * capacity + width :]
    near = near + lax.ppermute(far.astype(jnp.bfloat16), "expert", across).astype(jnp.float32)
    near = near.astype(jnp.bfloat16)
    own_came = lax.ppermute(own_far.astype(jnp.bfloat16), "expert", across)
    pieces = [near[k * capacity : (k + 1) * capacity] for k in range(REACH - 1)]
    own = (own_near + after(own_came, *pieces).astype(jnp.float32)).astype(jnp.bfloat16)
    parts = [
        lax.ppermute(piece, ("section", "expert"), home(k + 1, onward))
        for k, piece in enumerate(pieces)
    ]
    parts.insert(0, lax.ppermute(own, ("section", "expert"), home(0, onward)))
    return jnp.concatenate(parts, axis=0)


def combine(placed, back, gate_values):
    picked = lax.dot_general(
        placed, back, (((0,), (0,)), ((), ())), preferred_element_type=jnp.float32
    )
    return picked * gate_values


def local(
    layer_input,
    cotangent,
    gate_weight,
    up_weight,
    down_weight,
    stashed_pre,
    first_ids,
    first_gates,
    second_ids,
    second_gates,
    keep_mask,
):
    devices = lax.axis_size("expert")
    sections = lax.axis_size("section")
    chips = devices // 2
    pairs = chips // 2
    capacity = stashed_pre.shape[2]
    slots = pairs * capacity
    hidden_local = gate_weight.shape[2]
    out, home, across, beside = routes(devices, sections)
    me = lax.axis_index("expert")
    chip, core = me // 2, me % 2
    tokens_in = layer_input[0]
    keep_rows = keep_mask[0]
    kept_grads = cotangent[0] * keep_rows[:, None].astype(jnp.bfloat16)
    first_at = places(first_ids[0], chip, pairs, capacity)
    second_at = places(second_ids[0], chip, pairs, capacity)
    ahead = [(i, (i + 1) % sections) for i in range(sections)]
    behind = [((i + 1) % sections, i) for i in range(sections)]
    origins = [
        [(here + jnp.where(here % 2 == 0, -step, step)) % chips for step in range(REACH)]
        for here in (chip, chip ^ 1)
    ]
    origins = [origins[0][0], origins[1][0], *origins[0][1:], *origins[1][1:]]
    stash_halves = [
        jnp.concatenate(
            [
                lax.dynamic_index_in_dim(stashed_pre[0], 2 * origin + which, 0, False)
                for origin in origins
            ]
        )
        for which in (core, 1 - core)
    ]
    gate_cols = gate_weight[0]
    up_cols = up_weight[0]
    down_rows = down_weight[0]

    held_first = dispatch(placement(first_at, slots), tokens_in, capacity, out, across)
    held_second = dispatch(placement(second_at, slots), kept_grads, capacity, out, across)
    beside_first = lax.ppermute(held_first, "expert", beside)
    relayed_tokens = lax.ppermute(after(tokens_in, held_first), "section", ahead)
    relayed_grads = lax.ppermute(after(cotangent[0], held_first), "section", behind)
    first_told = lax.ppermute(
        jnp.stack([after(first_at, held_first).astype(jnp.float32), first_gates[0, :, 0]]), "section", ahead
    )
    second_told = lax.ppermute(
        jnp.stack(
            [
                after(second_at, held_first).astype(jnp.float32),
                second_gates[0, :, 0],
                keep_rows.astype(jnp.float32),
            ]
        ),
        "section",
        behind,
    )
    first_mine = hidden_forward(held_first, gate_cols, up_cols)
    first_given = hidden_forward(beside_first, gate_cols, up_cols)
    first_mine, first_given = lax.optimization_barrier((first_mine, first_given))
    given_first = made_forward(first_given, down_rows)
    made_first = lax.optimization_barrier(made_forward(first_mine, down_rows))
    back_first = collect(
        made_first, given_first, capacity, 1, sections, home, across, beside
    )
    beside_second = lax.ppermute(held_second, "expert", beside)
    second_mine = hidden_backward(held_second, stash_halves[0], down_rows)
    second_given = hidden_backward(beside_second, stash_halves[1], down_rows)
    second_mine, second_given = lax.optimization_barrier((second_mine, second_given))
    given_second = made_backward(second_given, gate_cols, up_cols)
    made_second = lax.optimization_barrier(made_backward(second_mine, gate_cols, up_cols))
    back_second = collect(
        made_second, given_second, capacity, -1, sections, home, across, beside
    )
    first_branch = combine(
        placement(first_told[0].astype(jnp.int32), slots), back_first, first_told[1][:, None]
    )
    second_branch = combine(
        placement(second_told[0].astype(jnp.int32), slots), back_second, second_told[1][:, None]
    )
    mixed_out = (relayed_tokens.astype(jnp.float32) + first_branch).astype(jnp.bfloat16)
    grad_out = (
        second_told[2][:, None] * (relayed_grads.astype(jnp.float32) + second_branch)
    ).astype(jnp.bfloat16)
    return (mixed_out[None], grad_out[None])


def solution(mesh):
    placed = (
        P("section", "expert", None),
        P("section", "expert", None),
        P("section", None, "expert"),
        P("section", None, "expert"),
        P("section", "expert", None),
        P("section", None, None, None, "expert"),
        P("section", "expert", None),
        P("section", "expert", None),
        P("section", "expert", None),
        P("section", "expert", None),
        P("section", "expert"),
    )
    return jax.shard_map(
        local,
        mesh=mesh,
        in_specs=placed,
        out_specs=(P("section", "expert", None), P("section", "expert", None)),
        check_vma=False,
    )
```

```python
import functools

import jax
import jax.numpy as jnp
from jax import lax
from jax.experimental import pallas as pl
from jax.experimental.pallas import tpu as pltpu
from jax.sharding import PartitionSpec as P

REACH = 4


def routes(devices, sections):
    chips = devices // 2

    def nearer(step):
        for chip in range(chips):
            origin = (chip + (step if chip % 2 else -step)) % chips
            for core in range(2):
                yield 2 * origin + core, 2 * chip + core

    def out(step):
        return list(nearer(step))

    def home(step, onward):
        return [
            (s * devices + there, (s + onward) % sections * devices + origin)
            for s in range(sections)
            for origin, there in nearer(step)
        ]

    across = [(i, i ^ 2) for i in range(devices)]
    beside = [(i, i ^ 1) for i in range(devices)]
    return out, home, across, beside


def prepare_kernel(pairs, capacity, chip_ref, *refs):
    count = refs[0].shape[1]
    chip = chip_ref[0]
    odd = lax.rem(chip, 2)
    before = lax.broadcasted_iota(jnp.int32, (count, count), 0)
    before = (before < lax.broadcasted_iota(jnp.int32, (count, count), 1)).astype(jnp.bfloat16)

    def fill(ids, rows, keep, parts):
        ahead = ids - lax.div(chip, 2)
        ahead = jnp.where(ahead < 0, ahead + pairs, ahead)
        near = jnp.where(odd == 1, 1, pairs - 1)
        step = jnp.where(ahead == 0, 0, jnp.where(ahead == 2, 3, jnp.where(ahead == near, 1, 2)))
        chosen = lax.broadcasted_iota(jnp.int32, (8, count), 0) == step
        chosen = jnp.where(chosen, 1.0, 0.0)
        earlier = jnp.dot(
            chosen.astype(jnp.bfloat16), before, preferred_element_type=jnp.float32
        )
        slot = jnp.sum(chosen * earlier, axis=0, keepdims=True).astype(jnp.int32)
        place = step * capacity + slot
        for k, part in enumerate(parts):
            here = lax.broadcasted_iota(jnp.int32, (capacity, count), 0) + k * capacity == place
            here = jnp.where(here, keep, 0.0).astype(jnp.bfloat16)
            part[...] = jnp.dot(here, rows, preferred_element_type=jnp.float32).astype(part.dtype)
        return place.astype(jnp.float32)

    ids1, gates1, ids2, gates2, keep, rows1, rows2 = refs[:7]
    outs = refs[7:]
    kept = keep[...].astype(jnp.float32)
    outs[8][0:1, :] = fill(ids1[...], rows1[...], jnp.ones_like(kept), outs[:REACH])
    outs[8][1:2, :] = gates1[...]
    outs[9][0:1, :] = fill(ids2[...], rows2[...], kept, outs[REACH : 2 * REACH])
    outs[9][1:2, :] = gates2[...]
    outs[9][2:3, :] = kept


def prepare(chip, pairs, capacity, ids1, gates1, ids2, gates2, keep, rows1, rows2):
    count, width = rows1.shape
    piece = jax.ShapeDtypeStruct((capacity, width), jnp.bfloat16)
    whole = pl.BlockSpec(memory_space=pltpu.VMEM)
    made = pl.pallas_call(
        functools.partial(prepare_kernel, pairs, capacity),
        out_shape=[piece] * (2 * REACH)
        + [
            jax.ShapeDtypeStruct((2, count), jnp.float32),
            jax.ShapeDtypeStruct((3, count), jnp.float32),
        ],
        in_specs=[pl.BlockSpec(memory_space=pltpu.SMEM)] + [whole] * 7,
        out_specs=[whole] * (2 * REACH + 2),
        cost_estimate=pl.CostEstimate(
            flops=4 * REACH * capacity * count * width, bytes_accessed=8 * count * width, transcendentals=0
        ),
        name="prepare",
    )(chip[None], ids1, gates1, ids2, gates2, keep, rows1, rows2)
    return made[:REACH], made[REACH : 2 * REACH], made[8], made[9]


def placement(slot_at, slot_total):
    rows = lax.broadcasted_iota(jnp.int32, (slot_total, slot_at.shape[0]), 0)
    return (rows == slot_at[None, :]).astype(jnp.bfloat16)


def after(value, *others):
    return lax.optimization_barrier((value, *others))[0]


def hidden_forward(routed, gate_cols, up_cols):
    gate_pre = jnp.dot(routed, gate_cols, preferred_element_type=jnp.float32)
    up_pre = jnp.dot(routed, up_cols, preferred_element_type=jnp.float32)
    return ((jax.nn.silu(gate_pre) * up_pre).astype(jnp.bfloat16),)


def made_forward(hidden, down_rows):
    return jnp.dot(hidden[0], down_rows, preferred_element_type=jnp.float32).astype(jnp.bfloat16)


def hidden_backward(routed, stash_rows, down_rows):
    hidden_grad = jnp.dot(routed, down_rows.T, preferred_element_type=jnp.float32)
    gate_pre = stash_rows[:, 0, :].astype(jnp.float32)
    up_pre = stash_rows[:, 1, :].astype(jnp.float32)
    sigmoid_gate = jax.nn.sigmoid(gate_pre)
    grad_gate = (
        hidden_grad * up_pre * sigmoid_gate * (1.0 + gate_pre * (1.0 - sigmoid_gate))
    ).astype(jnp.bfloat16)
    grad_up = (hidden_grad * gate_pre * sigmoid_gate).astype(jnp.bfloat16)
    return grad_gate, grad_up


def made_backward(hidden, gate_cols, up_cols):
    total = jnp.dot(hidden[0], gate_cols.T, preferred_element_type=jnp.float32)
    total = total + jnp.dot(hidden[1], up_cols.T, preferred_element_type=jnp.float32)
    return total.astype(jnp.bfloat16)


def dispatch(pieces, out, across):
    own_distant = lax.ppermute(pieces[0], "expert", across)
    near = jnp.concatenate(
        [lax.ppermute(pieces[k], "expert", out(k)) for k in range(1, REACH)], axis=0
    )
    distant = lax.ppermute(near, "expert", across)
    return jnp.concatenate([pieces[0], own_distant, near, distant], axis=0), own_distant


def collect(mine, given, capacity, onward, sections, home, across, beside, earlier):
    came = lax.ppermute(given, "expert", beside)
    summed = mine.astype(jnp.float32) + came.astype(jnp.float32)
    own_near, own_far = summed[:capacity], summed[capacity : 2 * capacity]
    width = (REACH - 1) * capacity
    near, far = summed[2 * capacity : 2 * capacity + width], summed[2 * capacity + width :]
    far = after(far.astype(jnp.bfloat16), *earlier[0])
    near = near + lax.ppermute(far, "expert", across).astype(jnp.float32)
    near = after(near.astype(jnp.bfloat16), *earlier[1])
    own_came = lax.ppermute(own_far.astype(jnp.bfloat16), "expert", across)
    pieces = [near[k * capacity : (k + 1) * capacity] for k in range(REACH - 1)]
    own = (own_near + after(own_came, *pieces).astype(jnp.float32)).astype(jnp.bfloat16)
    parts = [
        lax.ppermute(piece, ("section", "expert"), home(k + 1, onward))
        for k, piece in enumerate(pieces)
    ]
    parts.insert(0, lax.ppermute(own, ("section", "expert"), home(0, onward)))
    return parts


def combine(placed, back, gate_values):
    picked = lax.dot_general(
        placed, back, (((0,), (0,)), ((), ())), preferred_element_type=jnp.float32
    )
    return picked * gate_values


def local(
    layer_input,
    cotangent,
    gate_weight,
    up_weight,
    down_weight,
    stashed_pre,
    first_ids,
    first_gates,
    second_ids,
    second_gates,
    keep_mask,
):
    devices = lax.axis_size("expert")
    sections = lax.axis_size("section")
    chips = devices // 2
    pairs = chips // 2
    capacity = stashed_pre.shape[2]
    slots = pairs * capacity
    hidden_local = gate_weight.shape[2]
    out, home, across, beside = routes(devices, sections)
    me = lax.axis_index("expert")
    chip, core = me // 2, me % 2
    ahead = [(i, (i + 1) % sections) for i in range(sections)]
    behind = [((i + 1) % sections, i) for i in range(sections)]
    first_pieces, second_pieces, first_told, second_told = prepare(
        chip,
        pairs,
        capacity,
        first_ids[..., 0],
        first_gates[..., 0],
        second_ids[..., 0],
        second_gates[..., 0],
        keep_mask,
        layer_input[0],
        cotangent[0],
    )
    origins = [
        [(here + jnp.where(here % 2 == 0, -step, step)) % chips for step in range(REACH)]
        for here in (chip, chip ^ 1)
    ]
    origins = [origins[0][0], origins[1][0], *origins[0][1:], *origins[1][1:]]
    stash_halves = [
        jnp.concatenate(
            [
                lax.dynamic_index_in_dim(stashed_pre[0], 2 * origin + which, 0, False)
                for origin in origins
            ]
        )
        for which in (core, 1 - core)
    ]
    gate_cols = gate_weight[0]
    up_cols = up_weight[0]
    down_rows = down_weight[0]

    held_first, own_distant = dispatch(first_pieces, out, across)
    second_pieces = lax.optimization_barrier((*second_pieces, own_distant))[:REACH]
    held_second, _ = dispatch(second_pieces, out, across)
    tokens, grads, first_told, second_told, _ = lax.optimization_barrier(
        (layer_input[0], cotangent[0], first_told, second_told, held_first)
    )
    first_told = lax.ppermute(first_told, "section", ahead)
    second_told = lax.ppermute(second_told, "section", behind)
    tokens = lax.ppermute(tokens, "section", ahead)
    grads = lax.ppermute(grads, "section", behind)
    beside_first = lax.ppermute(held_first, "expert", beside)
    first_mine = hidden_forward(held_first, gate_cols, up_cols)
    first_given = hidden_forward(beside_first, gate_cols, up_cols)
    first_mine, first_given = lax.optimization_barrier((first_mine, first_given))
    given_first = made_forward(first_given, down_rows)
    made_first = lax.optimization_barrier(made_forward(first_mine, down_rows))
    back_first = collect(
        made_first, given_first, capacity, 1, sections, home, across, beside, ((), ())
    )
    held_second = after(held_second, made_first, given_first)
    beside_second = lax.ppermute(held_second, "expert", beside)
    second_mine = hidden_backward(held_second, stash_halves[0], down_rows)
    second_given = hidden_backward(beside_second, stash_halves[1], down_rows)
    second_mine, second_given = lax.optimization_barrier((second_mine, second_given))
    given_second = made_backward(second_given, gate_cols, up_cols)
    made_second = lax.optimization_barrier(made_backward(second_mine, gate_cols, up_cols))
    back_second = collect(
        made_second,
        given_second,
        capacity,
        -1,
        sections,
        home,
        across,
        beside,
        ((tokens, grads, first_told, second_told), back_first),
    )
    first_branch = combine(
        placement(first_told[0].astype(jnp.int32), slots), jnp.concatenate(back_first), first_told[1][:, None]
    )
    second_branch = combine(
        placement(second_told[0].astype(jnp.int32), slots), jnp.concatenate(back_second), second_told[1][:, None]
    )
    mixed_out = (tokens.astype(jnp.float32) + first_branch).astype(jnp.bfloat16)
    grad_out = (
        second_told[2][:, None] * (grads.astype(jnp.float32) + second_branch)
    ).astype(jnp.bfloat16)
    return (mixed_out[None], grad_out[None])


def solution(mesh):
    placed = (
        P("section", "expert", None),
        P("section", "expert", None),
        P("section", None, "expert"),
        P("section", None, "expert"),
        P("section", "expert", None),
        P("section", None, None, None, "expert"),
        P("section", "expert", None),
        P("section", "expert", None),
        P("section", "expert", None),
        P("section", "expert", None),
        P("section", "expert"),
    )
    return jax.shard_map(
        local,
        mesh=mesh,
        in_specs=placed,
        out_specs=(P("section", "expert", None), P("section", "expert", None)),
        check_vma=False,
    )
```

```python
import functools

import jax
import jax.numpy as jnp
from jax import lax
from jax.experimental import pallas as pl
from jax.experimental.pallas import tpu as pltpu
from jax.sharding import PartitionSpec as P

REACH = 4
EDGES = [['jB', 'own_d'], ['fwdB', 'rB'], ['relayB', 'jB1'], ['gF', 'rB'], ['heldF', 'closeB'], ['mF', 'gF'], ['distB', 'gF'], ['homeF', 'payB'], ['homeB', 'h2F'], ['homeB', 'h3F']]
RELAY = 0
MERGE = True


def routes(devices, sections):
    chips = devices // 2

    def nearer(step):
        for chip in range(chips):
            origin = (chip + (step if chip % 2 else -step)) % chips
            for core in range(2):
                yield 2 * origin + core, 2 * chip + core

    def out(step):
        return list(nearer(step))

    def home(step, onward):
        return [
            (s * devices + there, (s + onward) % sections * devices + origin)
            for s in range(sections)
            for origin, there in nearer(step)
        ]

    across = [(i, i ^ 2) for i in range(devices)]
    beside = [(i, i ^ 1) for i in range(devices)]
    return out, home, across, beside


def prepare_kernel(pairs, capacity, chip_ref, *refs):
    count = refs[0].shape[1]
    chip = chip_ref[0]
    odd = lax.rem(chip, 2)
    before = lax.broadcasted_iota(jnp.int32, (count, count), 0)
    before = (before < lax.broadcasted_iota(jnp.int32, (count, count), 1)).astype(jnp.bfloat16)

    def fill(ids, rows, keep, parts):
        ahead = ids - lax.div(chip, 2)
        ahead = jnp.where(ahead < 0, ahead + pairs, ahead)
        near = jnp.where(odd == 1, 1, pairs - 1)
        step = jnp.where(ahead == 0, 0, jnp.where(ahead == 2, 3, jnp.where(ahead == near, 1, 2)))
        chosen = lax.broadcasted_iota(jnp.int32, (8, count), 0) == step
        chosen = jnp.where(chosen, 1.0, 0.0)
        earlier = jnp.dot(
            chosen.astype(jnp.bfloat16), before, preferred_element_type=jnp.float32
        )
        slot = jnp.sum(chosen * earlier, axis=0, keepdims=True).astype(jnp.int32)
        place = step * capacity + slot
        for k, (part, start) in enumerate(parts):
            here = lax.broadcasted_iota(jnp.int32, (capacity, count), 0) + k * capacity == place
            here = jnp.where(here, keep, 0.0).astype(jnp.bfloat16)
            made = jnp.dot(here, rows, preferred_element_type=jnp.float32)
            part[start : start + capacity, :] = made.astype(part.dtype)
        return place.astype(jnp.float32)

    ids1, gates1, ids2, gates2, keep, rows1, rows2 = refs[:7]
    own, near1, near2, told1, told2 = refs[7], refs[8:11], refs[11:14], refs[14], refs[15]
    kept = keep[...].astype(jnp.float32)
    parts1 = [(own, 0)] + [(part, 0) for part in near1]
    parts2 = [(own, capacity)] + [(part, 0) for part in near2]
    place1 = fill(ids1[...], rows1[...], jnp.ones_like(kept), parts1)
    place2 = fill(ids2[...], rows2[...], kept, parts2)

    def tell(told, place, gates):
        high = gates.astype(jnp.bfloat16).astype(jnp.float32)
        middle = (gates - high).astype(jnp.bfloat16).astype(jnp.float32)
        low = gates - high - middle
        row = lax.broadcasted_iota(jnp.int32, (8, count), 0)
        lines = jnp.zeros((8, count), jnp.float32)
        for k, line in enumerate((place, high, middle, low, kept)):
            lines = jnp.where(row == k, line, lines)
        told[...] = jnp.zeros_like(told)
        told[:, 0:count] = lines.astype(told.dtype)

    tell(told1, place1, gates1[...])
    tell(told2, place2, gates2[...])


def prepare(chip, pairs, capacity, ids1, gates1, ids2, gates2, keep, rows1, rows2):
    count, width = rows1.shape
    piece = jax.ShapeDtypeStruct((capacity, width), jnp.bfloat16)
    whole = pl.BlockSpec(memory_space=pltpu.VMEM)
    made = pl.pallas_call(
        functools.partial(prepare_kernel, pairs, capacity),
        out_shape=[jax.ShapeDtypeStruct((2 * capacity, width), jnp.bfloat16)]
        + [piece] * (2 * REACH - 2)
        + [
            jax.ShapeDtypeStruct((8, width), jnp.bfloat16),
            jax.ShapeDtypeStruct((8, width), jnp.bfloat16),
        ],
        in_specs=[pl.BlockSpec(memory_space=pltpu.SMEM)] + [whole] * 7,
        out_specs=[whole] * (2 * REACH + 1),
        cost_estimate=pl.CostEstimate(
            flops=4 * REACH * capacity * count * width, bytes_accessed=8 * count * width, transcendentals=0
        ),
        name="prepare",
    )(chip[None], ids1, gates1, ids2, gates2, keep, rows1, rows2)
    return made[0], made[1:REACH], made[REACH : 2 * REACH - 1], made[-2], made[-1]


def placement(slot_at, slot_total):
    rows = lax.broadcasted_iota(jnp.int32, (slot_total, slot_at.shape[0]), 0)
    return (rows == slot_at[None, :]).astype(jnp.bfloat16)


def after(value, *others):
    return lax.optimization_barrier((value, *others))[0]


def hidden_forward(routed, gate_cols, up_cols):
    gate_pre = jnp.dot(routed, gate_cols, preferred_element_type=jnp.float32)
    up_pre = jnp.dot(routed, up_cols, preferred_element_type=jnp.float32)
    return ((jax.nn.silu(gate_pre) * up_pre).astype(jnp.bfloat16),)


def made_forward(hidden, down_rows):
    return jnp.dot(hidden[0], down_rows, preferred_element_type=jnp.float32).astype(jnp.bfloat16)


def hidden_backward(routed, stash_rows, down_rows):
    hidden_grad = jnp.dot(routed, down_rows.T, preferred_element_type=jnp.float32)
    gate_pre = stash_rows[:, 0, :].astype(jnp.float32)
    up_pre = stash_rows[:, 1, :].astype(jnp.float32)
    sigmoid_gate = jax.nn.sigmoid(gate_pre)
    grad_gate = (
        hidden_grad * up_pre * sigmoid_gate * (1.0 + gate_pre * (1.0 - sigmoid_gate))
    ).astype(jnp.bfloat16)
    grad_up = (hidden_grad * gate_pre * sigmoid_gate).astype(jnp.bfloat16)
    return grad_gate, grad_up


def made_backward(hidden, gate_cols, up_cols):
    total = jnp.dot(hidden[0], gate_cols.T, preferred_element_type=jnp.float32)
    total = total + jnp.dot(hidden[1], up_cols.T, preferred_element_type=jnp.float32)
    return total.astype(jnp.bfloat16)


def collect(mine, came, capacity, onward, home):
    summed = mine.astype(jnp.float32) + came.astype(jnp.float32)
    width = 2 * capacity

    def sent(k):
        return summed[(REACH + k) * capacity :][:width].astype(jnp.bfloat16)

    def kept(k, arrived):
        total = summed[k * capacity :][:width] + arrived.astype(jnp.float32)
        return total.astype(jnp.bfloat16)

    def homeward(pieces, k):
        return [
            lax.ppermute(pieces[i * capacity :][:capacity], ("section", "expert"), home(k + i, onward))
            for i in (1, 0)
        ][::-1]

    return sent, kept, homeward


def combine(placed, back, gate_values):
    picked = lax.dot_general(
        placed, back, (((0,), (0,)), ((), ())), preferred_element_type=jnp.float32
    )
    return picked * gate_values


def local(
    layer_input,
    cotangent,
    gate_weight,
    up_weight,
    down_weight,
    stashed_pre,
    first_ids,
    first_gates,
    second_ids,
    second_gates,
    keep_mask,
):
    devices = lax.axis_size("expert")
    sections = lax.axis_size("section")
    chips = devices // 2
    pairs = chips // 2
    capacity = stashed_pre.shape[2]
    slots = pairs * capacity
    hidden_local = gate_weight.shape[2]
    out, home, across, beside = routes(devices, sections)
    me = lax.axis_index("expert")
    chip, core = me // 2, me % 2
    ahead = [(i, (i + 1) % sections) for i in range(sections)]
    behind = [((i + 1) % sections, i) for i in range(sections)]
    own_pieces, first_near, second_near, first_told, second_told = prepare(
        chip,
        pairs,
        capacity,
        first_ids[..., 0],
        first_gates[..., 0],
        second_ids[..., 0],
        second_gates[..., 0],
        keep_mask,
        layer_input[0],
        cotangent[0],
    )
    origins = [
        [(here + jnp.where(here % 2 == 0, -step, step)) % chips for step in range(REACH)]
        for here in (chip, chip ^ 1)
    ]
    origins = origins[0] + origins[1]
    stash_halves = [
        jnp.concatenate(
            [
                lax.dynamic_index_in_dim(stashed_pre[0], 2 * origin + which, 0, False)
                for origin in origins
            ]
        )
        for which in (core, 1 - core)
    ]
    gate_cols = gate_weight[0]
    up_cols = up_weight[0]
    down_rows = down_weight[0]

    V = {}

    def gate(name, value):
        for target, source in EDGES:
            if target == name:
                value = after(value, V[source])
        return value

    V["own_d"] = own_distant = lax.ppermute(own_pieces, "expert", across)
    first_near = [
        lax.ppermute(gate(f"jF{k + 1}", piece), "expert", out(k + 1)) for k, piece in enumerate(first_near)
    ]
    V["jF1"], V["jF2"], V["jF3"] = first_near
    second_near = [gate(f"jB{k + 1}", gate("jB", piece)) for k, piece in enumerate(second_near)]
    second_near = [
        lax.ppermute(piece, "expert", out(k + 1)) for k, piece in enumerate(second_near)
    ]
    V["jB1"], V["jB2"], V["jB3"] = second_near
    first_close = gate("fwdF", jnp.concatenate(first_near))
    first_distant = lax.ppermute(first_close, "expert", across)
    V["fwdF"] = first_distant
    relay_done = False

    bundles = [
        jnp.concatenate((rows[0], told))
        for rows, told in ((layer_input, first_told), (cotangent, second_told))
    ]

    def relay(first, second):
        if not MERGE:
            first = lax.ppermute(gate("relayF", first), "section", ahead)
            V["rF"] = first
        V["rB"] = second = lax.ppermute(gate("relayB", second), "section", behind)
        return first, second

    told = bundles
    if RELAY == 0:
        told = relay(*told)
    V["closeB"] = second_close = gate("fwdB", jnp.concatenate(second_near))
    second_distant = lax.ppermute(second_close, "expert", across)
    V["fwdB"] = second_distant
    if RELAY == 1:
        told = relay(*told)
    held_first = jnp.concatenate(
        [own_pieces[:capacity], *first_near, own_distant[:capacity], first_distant]
    )
    V["heldF"] = held_first = gate("heldF", held_first)
    if RELAY == 2:
        told = relay(*told)
    beside_first = lax.ppermute(held_first, "expert", beside)
    V["coreF"] = beside_first
    first_mine = hidden_forward(gate("hmF", held_first), gate_cols, up_cols)
    V["hmF"] = first_mine[0]
    if RELAY == 3:
        told = relay(*told)
    first_given = hidden_forward(gate("hgF", beside_first), gate_cols, up_cols)
    V["hgF"] = first_given[0]
    first_mine, first_given = lax.optimization_barrier((first_mine, first_given))
    given_first = made_forward((gate("gF", first_given[0]),), down_rows)
    V["gF"] = given_first
    if RELAY == 4:
        told = relay(*told)
    came_first = lax.ppermute(given_first, "expert", beside)
    V["cF"] = came_first
    made_first = lax.optimization_barrier(made_forward((gate("mF", first_mine[0]),), down_rows))
    V["mF"] = made_first

    second_distant = gate("distB", second_distant)
    held_second = jnp.concatenate(
        [own_pieces[capacity:], *second_near, own_distant[capacity:], second_distant]
    )
    V["heldB"] = held_second = gate("heldB", held_second)
    beside_second = lax.ppermute(held_second, "expert", beside)
    V["coreB"] = beside_second
    second_mine = hidden_backward(gate("hmB", held_second), stash_halves[0], down_rows)
    V["hmB"] = second_mine[0]
    second_given = hidden_backward(gate("hgB", beside_second), stash_halves[1], down_rows)
    second_mine, second_given = lax.optimization_barrier((second_mine, second_given))
    given_second = made_backward(second_given, gate_cols, up_cols)
    V["gB"] = given_second
    came_second = lax.ppermute(given_second, "expert", beside)
    V["cB"] = came_second
    second_mine = (gate("mB", second_mine[0]), second_mine[1])
    made_second = lax.optimization_barrier(made_backward(second_mine, gate_cols, up_cols))

    sent, kept, homeward = collect(made_first, came_first, capacity, 1, home)
    sent2, kept2, homeward2 = collect(made_second, came_second, capacity, -1, home)
    far = lax.ppermute(gate("farF", sent(2)), "expert", across)
    V["farF"] = far
    if RELAY == 5:
        told = relay(*told)
    V["payB"] = far2 = gate("farB", sent2(2))
    short = lax.ppermute(gate("shortF", sent(0)), "expert", across)
    V["shortF"] = short
    V["piecesF"] = pieces = gate("homeF", kept(2, far))
    back_first = homeward(pieces, 2)
    V["h2F"], V["h3F"] = back_first
    far2 = lax.ppermute(far2, "expert", across)
    V["farB"] = far2
    last = gate("home0F", kept(0, after(short, pieces)))
    if MERGE:
        bundle = jnp.concatenate((last[:capacity], bundles[0]))
        bundle = lax.ppermute(bundle, ("section", "expert"), home(0, 1))
        one = lax.ppermute(last[capacity:], ("section", "expert"), home(1, 1))
        back_first = [bundle[:capacity], one] + back_first
        told = (bundle[capacity:], told[1])
    else:
        back_first = homeward(last, 0) + back_first
    V["h0F"], V["h1F"] = back_first[:2]
    short2 = lax.ppermute(gate("shortB", sent2(0)), "expert", across)
    pieces = gate("homeB", kept2(2, far2))
    back_second = homeward2(pieces, 2)
    V["h2B"], V["h3B"] = back_second
    pieces = gate("home0B", kept2(0, after(short2, pieces)))
    back_second = homeward2(pieces, 0) + back_second
    count = layer_input.shape[1]

    def unpack(bundle, back):
        lines = bundle[count:, :count].astype(jnp.float32)
        gates = (lines[1] + lines[2]) + lines[3]
        rows = jnp.concatenate(back)
        branch = combine(placement(lines[0].astype(jnp.int32), slots), rows, gates[:, None])
        return branch, bundle[:count].astype(jnp.float32), lines[4][:, None]

    first_branch, tokens, _ = unpack(told[0], back_first)
    second_branch, grads, keep = unpack(told[1], back_second)
    mixed_out = (tokens + first_branch).astype(jnp.bfloat16)
    grad_out = (keep * (grads + second_branch)).astype(jnp.bfloat16)
    return (mixed_out[None], grad_out[None])


def solution(mesh):
    placed = (
        P("section", "expert", None),
        P("section", "expert", None),
        P("section", None, "expert"),
        P("section", None, "expert"),
        P("section", "expert", None),
        P("section", None, None, None, "expert"),
        P("section", "expert", None),
        P("section", "expert", None),
        P("section", "expert", None),
        P("section", "expert", None),
        P("section", "expert"),
    )
    return jax.shard_map(
        local,
        mesh=mesh,
        in_specs=placed,
        out_specs=(P("section", "expert", None), P("section", "expert", None)),
        check_vma=False,
    )
```

```python
import functools

import jax
import jax.numpy as jnp
from jax import lax
from jax.experimental import pallas as pl
from jax.experimental.pallas import tpu as pltpu
from jax.sharding import PartitionSpec as P

REACH = 4
EDGES = [['jB', 'own_d'], ['heldB', 'rB'], ['heldB', 'rF'], ['heldF', 'closeB'], ['mF', 'gF'], ['distB', 'gF'], ['homeF', 'payB'], ['shortB', 'h3F'], ['home0B', 'h0F'], ['home0B', 'h1F'], ['home0F', 'payB'], ['ownB', 'own_d']]
RELAY = 3
MERGE = False
OWN = 1


def routes(devices, sections):
    chips = devices // 2

    def nearer(step):
        for chip in range(chips):
            origin = (chip + (step if chip % 2 else -step)) % chips
            for core in range(2):
                yield 2 * origin + core, 2 * chip + core

    def out(step):
        return list(nearer(step))

    def home(step, onward):
        return [
            (s * devices + there, (s + onward) % sections * devices + origin)
            for s in range(sections)
            for origin, there in nearer(step)
        ]

    across = [(i, i ^ 2) for i in range(devices)]
    beside = [(i, i ^ 1) for i in range(devices)]
    return out, home, across, beside


def prepare_kernel(pairs, capacity, masked, chip_ref, ids_ref, gates_ref, keep_ref, rows_ref, *outs):
    count, rows = ids_ref.shape[1], rows_ref[...]
    chip = chip_ref[0]
    kept = keep_ref[...].astype(jnp.float32)
    before = lax.broadcasted_iota(jnp.int32, (count, count), 0)
    before = (before < lax.broadcasted_iota(jnp.int32, (count, count), 1)).astype(jnp.bfloat16)
    ahead = ids_ref[...] - lax.div(chip, 2)
    ahead = jnp.where(ahead < 0, ahead + pairs, ahead)
    near = jnp.where(lax.rem(chip, 2) == 1, 1, pairs - 1)
    step = jnp.where(ahead == 0, 0, jnp.where(ahead == 2, 3, jnp.where(ahead == near, 1, 2)))
    chosen = jnp.where(lax.broadcasted_iota(jnp.int32, (8, count), 0) == step, 1.0, 0.0)
    earlier = jnp.dot(chosen.astype(jnp.bfloat16), before, preferred_element_type=jnp.float32)
    slot = jnp.sum(chosen * earlier, axis=0, keepdims=True).astype(jnp.int32)
    place = step * capacity + slot
    for k in range(REACH):
        here = lax.broadcasted_iota(jnp.int32, (capacity, count), 0) + k * capacity == place
        here = jnp.where(here, kept if masked else 1.0, 0.0).astype(jnp.bfloat16)
        made = jnp.dot(here, rows, preferred_element_type=jnp.float32)
        outs[k][...] = made.astype(jnp.bfloat16)
    gates = gates_ref[...]
    high = gates.astype(jnp.bfloat16).astype(jnp.float32)
    middle = (gates - high).astype(jnp.bfloat16).astype(jnp.float32)
    row = lax.broadcasted_iota(jnp.int32, (8, count), 0)
    lines = jnp.zeros((8, count), jnp.float32)
    for k, line in enumerate((place.astype(jnp.float32), high, middle, gates - high - middle, kept)):
        lines = jnp.where(row == k, line, lines)
    told = outs[REACH]
    told[...] = jnp.zeros_like(told)
    told[:, 0:count] = lines.astype(told.dtype)


def prepare(masked, chip, pairs, capacity, ids, gates, keep, rows):
    count, width = rows.shape
    whole = pl.BlockSpec(memory_space=pltpu.VMEM)
    made = pl.pallas_call(
        functools.partial(prepare_kernel, pairs, capacity, masked),
        out_shape=[jax.ShapeDtypeStruct((capacity, width), jnp.bfloat16)] * REACH
        + [jax.ShapeDtypeStruct((8, width), jnp.bfloat16)],
        in_specs=[pl.BlockSpec(memory_space=pltpu.SMEM)] + [whole] * 4,
        out_specs=[whole] * (REACH + 1),
        cost_estimate=pl.CostEstimate(
            flops=2 * REACH * capacity * count * width,
            bytes_accessed=4 * count * width,
            transcendentals=0,
        ),
        name="prepare_second" if masked else "prepare_first",
    )(chip[None], ids, gates, keep, rows)
    return made[:REACH], made[REACH]


def placement(slot_at, slot_total):
    rows = lax.broadcasted_iota(jnp.int32, (slot_total, slot_at.shape[0]), 0)
    return (rows == slot_at[None, :]).astype(jnp.bfloat16)


def after(value, *others):
    return lax.optimization_barrier((value, *others))[0]


def hidden_forward(routed, gate_cols, up_cols):
    gate_pre = jnp.dot(routed, gate_cols, preferred_element_type=jnp.float32)
    up_pre = jnp.dot(routed, up_cols, preferred_element_type=jnp.float32)
    return ((jax.nn.silu(gate_pre) * up_pre).astype(jnp.bfloat16),)


def made_forward(hidden, down_rows):
    return jnp.dot(hidden[0], down_rows, preferred_element_type=jnp.float32).astype(jnp.bfloat16)


def hidden_backward(routed, stash_rows, down_rows):
    hidden_grad = jnp.dot(routed, down_rows.T, preferred_element_type=jnp.float32)
    gate_pre = stash_rows[:, 0, :].astype(jnp.float32)
    up_pre = stash_rows[:, 1, :].astype(jnp.float32)
    sigmoid_gate = jax.nn.sigmoid(gate_pre)
    grad_gate = (
        hidden_grad * up_pre * sigmoid_gate * (1.0 + gate_pre * (1.0 - sigmoid_gate))
    ).astype(jnp.bfloat16)
    grad_up = (hidden_grad * gate_pre * sigmoid_gate).astype(jnp.bfloat16)
    return grad_gate, grad_up


def made_backward(hidden, gate_cols, up_cols):
    total = jnp.dot(hidden[0], gate_cols.T, preferred_element_type=jnp.float32)
    total = total + jnp.dot(hidden[1], up_cols.T, preferred_element_type=jnp.float32)
    return total.astype(jnp.bfloat16)


def collect(mine, came, capacity, onward, home):
    summed = mine.astype(jnp.float32) + came.astype(jnp.float32)
    width = 2 * capacity

    def sent(k):
        return summed[(REACH + k) * capacity :][:width].astype(jnp.bfloat16)

    def kept(k, arrived):
        total = summed[k * capacity :][:width] + arrived.astype(jnp.float32)
        return total.astype(jnp.bfloat16)

    def homeward(pieces, k):
        return [
            lax.ppermute(pieces[i * capacity :][:capacity], ("section", "expert"), home(k + i, onward))
            for i in (1, 0)
        ][::-1]

    return sent, kept, homeward


def combine(placed, back, gate_values):
    picked = lax.dot_general(
        placed, back, (((0,), (0,)), ((), ())), preferred_element_type=jnp.float32
    )
    return picked * gate_values


def local(
    layer_input,
    cotangent,
    gate_weight,
    up_weight,
    down_weight,
    stashed_pre,
    first_ids,
    first_gates,
    second_ids,
    second_gates,
    keep_mask,
):
    devices = lax.axis_size("expert")
    sections = lax.axis_size("section")
    chips = devices // 2
    pairs = chips // 2
    capacity = stashed_pre.shape[2]
    slots = pairs * capacity
    hidden_local = gate_weight.shape[2]
    out, home, across, beside = routes(devices, sections)
    me = lax.axis_index("expert")
    chip, core = me // 2, me % 2
    ahead = [(i, (i + 1) % sections) for i in range(sections)]
    behind = [((i + 1) % sections, i) for i in range(sections)]
    first_pieces, first_told = prepare(
        False, chip, pairs, capacity, first_ids[..., 0], first_gates[..., 0], keep_mask, layer_input[0]
    )
    second_pieces, second_told = prepare(
        True, chip, pairs, capacity, second_ids[..., 0], second_gates[..., 0], keep_mask, cotangent[0]
    )
    first_near, second_near = first_pieces[1:], second_pieces[1:]
    origins = [
        [(here + jnp.where(here % 2 == 0, -step, step)) % chips for step in range(REACH)]
        for here in (chip, chip ^ 1)
    ]
    origins = origins[0] + origins[1]
    stash_halves = [
        jnp.concatenate(
            [
                lax.dynamic_index_in_dim(stashed_pre[0], 2 * origin + which, 0, False)
                for origin in origins
            ]
        )
        for which in (core, 1 - core)
    ]
    gate_cols = gate_weight[0]
    up_cols = up_weight[0]
    down_rows = down_weight[0]

    V = {}

    def gate(name, value):
        for target, source in EDGES:
            if target == name:
                value = after(value, V[source])
        return value

    if OWN == 0:
        own_pieces = jnp.concatenate((first_pieces[0], second_pieces[0]))
        V["own_d"] = own_distant = lax.ppermute(own_pieces, "expert", across)
        own_distants = own_distant[:capacity], own_distant[capacity:]
    else:
        V["own_d"] = lax.ppermute(first_pieces[0], "expert", across)
    first_near = [
        lax.ppermute(gate(f"jF{k + 1}", piece), "expert", out(k + 1)) for k, piece in enumerate(first_near)
    ]
    V["jF1"], V["jF2"], V["jF3"] = first_near
    if OWN == 1:
        own_distants = V["own_d"], lax.ppermute(gate("ownB", second_pieces[0]), "expert", across)
        V["own_dB"] = own_distants[1]
    second_near = [gate(f"jB{k + 1}", gate("jB", piece)) for k, piece in enumerate(second_near)]
    second_near = [
        lax.ppermute(piece, "expert", out(k + 1)) for k, piece in enumerate(second_near)
    ]
    V["jB1"], V["jB2"], V["jB3"] = second_near
    first_close = gate("fwdF", jnp.concatenate(first_near))
    first_distant = lax.ppermute(first_close, "expert", across)
    V["fwdF"] = first_distant
    relay_done = False

    bundles = [
        jnp.concatenate((rows[0], told))
        for rows, told in ((layer_input, first_told), (cotangent, second_told))
    ]

    def relay(first, second):
        if not MERGE:
            first = lax.ppermute(gate("relayF", first), "section", ahead)
            V["rF"] = first
        V["rB"] = second = lax.ppermute(gate("relayB", second), "section", behind)
        return first, second

    told = bundles
    if RELAY == 0:
        told = relay(*told)
    V["closeB"] = second_close = gate("fwdB", jnp.concatenate(second_near))
    second_distant = lax.ppermute(second_close, "expert", across)
    V["fwdB"] = second_distant
    if RELAY == 1:
        told = relay(*told)
    held_first = jnp.concatenate(
        [first_pieces[0], *first_near, own_distants[0], first_distant]
    )
    V["heldF"] = held_first = gate("heldF", held_first)
    if RELAY == 2:
        told = relay(*told)
    beside_first = lax.ppermute(held_first, "expert", beside)
    V["coreF"] = beside_first
    first_mine = hidden_forward(gate("hmF", held_first), gate_cols, up_cols)
    V["hmF"] = first_mine[0]
    if RELAY == 3:
        told = relay(*told)
    first_given = hidden_forward(gate("hgF", beside_first), gate_cols, up_cols)
    V["hgF"] = first_given[0]
    first_mine, first_given = lax.optimization_barrier((first_mine, first_given))
    given_first = made_forward((gate("gF", first_given[0]),), down_rows)
    V["gF"] = given_first
    if RELAY == 4:
        told = relay(*told)
    came_first = lax.ppermute(given_first, "expert", beside)
    V["cF"] = came_first
    made_first = lax.optimization_barrier(made_forward((gate("mF", first_mine[0]),), down_rows))
    V["mF"] = made_first

    sent, kept, homeward = collect(made_first, came_first, capacity, 1, home)
    V["payF"] = far = gate("farF", sent(2))
    second_distant = gate("distB", second_distant)
    held_second = jnp.concatenate(
        [second_pieces[0], *second_near, own_distants[1], second_distant]
    )
    V["heldB"] = held_second = gate("heldB", held_second)
    beside_second = lax.ppermute(held_second, "expert", beside)
    V["coreB"] = beside_second
    second_mine = hidden_backward(gate("hmB", held_second), stash_halves[0], down_rows)
    V["hmB"] = second_mine[0]
    second_given = hidden_backward(gate("hgB", beside_second), stash_halves[1], down_rows)
    second_mine, second_given = lax.optimization_barrier((second_mine, second_given))
    given_second = made_backward(second_given, gate_cols, up_cols)
    V["gB"] = given_second
    came_second = lax.ppermute(given_second, "expert", beside)
    V["cB"] = came_second
    second_mine = (gate("mB", second_mine[0]), second_mine[1])
    made_second = lax.optimization_barrier(made_backward(second_mine, gate_cols, up_cols))

    sent2, kept2, homeward2 = collect(made_second, came_second, capacity, -1, home)
    far = lax.ppermute(far, "expert", across)
    V["farF"] = far
    if RELAY == 5:
        told = relay(*told)
    V["payB"] = far2 = gate("farB", sent2(2))
    short = lax.ppermute(gate("shortF", sent(0)), "expert", across)
    V["shortF"] = short
    V["piecesF"] = pieces = gate("homeF", kept(2, far))
    back_first = homeward(pieces, 2)
    V["h2F"], V["h3F"] = back_first
    far2 = lax.ppermute(far2, "expert", across)
    V["farB"] = far2
    last = gate("home0F", kept(0, after(short, pieces)))
    if MERGE:
        bundle = jnp.concatenate((last[:capacity], bundles[0]))
        bundle = lax.ppermute(bundle, ("section", "expert"), home(0, 1))
        one = lax.ppermute(last[capacity:], ("section", "expert"), home(1, 1))
        back_first = [bundle[:capacity], one] + back_first
        told = (bundle[capacity:], told[1])
    else:
        back_first = homeward(last, 0) + back_first
    V["h0F"], V["h1F"] = back_first[:2]
    short2 = lax.ppermute(gate("shortB", sent2(0)), "expert", across)
    pieces = gate("homeB", kept2(2, far2))
    back_second = homeward2(pieces, 2)
    V["h2B"], V["h3B"] = back_second
    pieces = gate("home0B", kept2(0, after(short2, pieces)))
    back_second = homeward2(pieces, 0) + back_second
    count = layer_input.shape[1]

    def unpack(bundle, back):
        lines = bundle[count:, :count].astype(jnp.float32)
        gates = (lines[1] + lines[2]) + lines[3]
        rows = jnp.concatenate(back)
        branch = combine(placement(lines[0].astype(jnp.int32), slots), rows, gates[:, None])
        return branch, bundle[:count].astype(jnp.float32), lines[4][:, None]

    first_branch, tokens, _ = unpack(told[0], back_first)
    second_branch, grads, keep = unpack(told[1], back_second)
    mixed_out = (tokens + first_branch).astype(jnp.bfloat16)
    grad_out = (keep * (grads + second_branch)).astype(jnp.bfloat16)
    return (mixed_out[None], grad_out[None])


def solution(mesh):
    placed = (
        P("section", "expert", None),
        P("section", "expert", None),
        P("section", None, "expert"),
        P("section", None, "expert"),
        P("section", "expert", None),
        P("section", None, None, None, "expert"),
        P("section", "expert", None),
        P("section", "expert", None),
        P("section", "expert", None),
        P("section", "expert", None),
        P("section", "expert"),
    )
    return jax.shard_map(
        local,
        mesh=mesh,
        in_specs=placed,
        out_specs=(P("section", "expert", None), P("section", "expert", None)),
        check_vma=False,
    )
```

```python
import functools

import jax
import jax.numpy as jnp
from jax import lax
from jax.experimental import pallas as pl
from jax.experimental.pallas import tpu as pltpu
from jax.sharding import PartitionSpec as P

REACH = 4
WAITS = (
    ("jB3", "own_d"),
    ("fwdF", "jB1"),
    ("relayB", "own_dB"),
    ("relayF", "own_dB"),
    ("heldB", "rB"),
    ("heldB", "rF"),
    ("heldF", "closeB"),
    ("mF", "gF"),
    ("distB", "gF"),
    ("homeF", "payB"),
    ("shortB", "h3F"),
    ("homeB", "h2F"),
    ("homeB", "h3F"),
    ("home0B", "h0F"),
    ("home0B", "h1F"),
    ("home0F", "payB"),
)


def routes(devices, sections):
    chips = devices // 2

    def nearer(step):
        for chip in range(chips):
            origin = (chip + (step if chip % 2 else -step)) % chips
            for core in range(2):
                yield 2 * origin + core, 2 * chip + core

    def out(step):
        return list(nearer(step))

    def home(step, onward):
        return [
            (s * devices + there, (s + onward) % sections * devices + origin)
            for s in range(sections)
            for origin, there in nearer(step)
        ]

    across = [(i, i ^ 2) for i in range(devices)]
    beside = [(i, i ^ 1) for i in range(devices)]
    return out, home, across, beside


def prepare_kernel(pairs, capacity, masked, chip_ref, ids_ref, gates_ref, keep_ref, rows_ref, *outs):
    count, rows = ids_ref.shape[1], rows_ref[...]
    chip = chip_ref[0]
    kept = keep_ref[...].astype(jnp.float32)
    before = lax.broadcasted_iota(jnp.int32, (count, count), 0)
    before = (before < lax.broadcasted_iota(jnp.int32, (count, count), 1)).astype(jnp.bfloat16)
    ahead = ids_ref[...] - lax.div(chip, 2)
    ahead = jnp.where(ahead < 0, ahead + pairs, ahead)
    near = jnp.where(lax.rem(chip, 2) == 1, 1, pairs - 1)
    step = jnp.where(ahead == 0, 0, jnp.where(ahead == 2, 3, jnp.where(ahead == near, 1, 2)))
    chosen = jnp.where(lax.broadcasted_iota(jnp.int32, (8, count), 0) == step, 1.0, 0.0)
    earlier = jnp.dot(chosen.astype(jnp.bfloat16), before, preferred_element_type=jnp.float32)
    slot = jnp.sum(chosen * earlier, axis=0, keepdims=True).astype(jnp.int32)
    place = step * capacity + slot
    for k in range(REACH):
        here = lax.broadcasted_iota(jnp.int32, (capacity, count), 0) + k * capacity == place
        here = jnp.where(here, kept if masked else 1.0, 0.0).astype(jnp.bfloat16)
        made = jnp.dot(here, rows, preferred_element_type=jnp.float32)
        outs[k][...] = made.astype(jnp.bfloat16)
    gates = gates_ref[...]
    high = gates.astype(jnp.bfloat16).astype(jnp.float32)
    middle = (gates - high).astype(jnp.bfloat16).astype(jnp.float32)
    row = lax.broadcasted_iota(jnp.int32, (8, count), 0)
    lines = jnp.zeros((8, count), jnp.float32)
    for k, line in enumerate((place.astype(jnp.float32), high, middle, gates - high - middle, kept)):
        lines = jnp.where(row == k, line, lines)
    told = outs[REACH]
    told[...] = jnp.zeros_like(told)
    told[:, 0:count] = lines.astype(told.dtype)


def prepare(masked, chip, pairs, capacity, ids, gates, keep, rows):
    count, width = rows.shape
    whole = pl.BlockSpec(memory_space=pltpu.VMEM)
    made = pl.pallas_call(
        functools.partial(prepare_kernel, pairs, capacity, masked),
        out_shape=[jax.ShapeDtypeStruct((capacity, width), jnp.bfloat16)] * REACH
        + [jax.ShapeDtypeStruct((8, width), jnp.bfloat16)],
        in_specs=[pl.BlockSpec(memory_space=pltpu.SMEM)] + [whole] * 4,
        out_specs=[whole] * (REACH + 1),
        cost_estimate=pl.CostEstimate(
            flops=2 * REACH * capacity * count * width,
            bytes_accessed=4 * count * width,
            transcendentals=0,
        ),
        name="prepare_second" if masked else "prepare_first",
    )(chip[None], ids, gates, keep, rows)
    return made[:REACH], made[REACH]


def placement(slot_at, slot_total):
    rows = lax.broadcasted_iota(jnp.int32, (slot_total, slot_at.shape[0]), 0)
    return (rows == slot_at[None, :]).astype(jnp.bfloat16)


def after(value, *others):
    return lax.optimization_barrier((value, *others))[0]


def hidden_forward(routed, gate_cols, up_cols):
    gate_pre = jnp.dot(routed, gate_cols, preferred_element_type=jnp.float32)
    up_pre = jnp.dot(routed, up_cols, preferred_element_type=jnp.float32)
    return ((jax.nn.silu(gate_pre) * up_pre).astype(jnp.bfloat16),)


def made_forward(hidden, down_rows):
    return jnp.dot(hidden[0], down_rows, preferred_element_type=jnp.float32).astype(jnp.bfloat16)


def hidden_backward(routed, stash_rows, down_rows):
    hidden_grad = jnp.dot(routed, down_rows.T, preferred_element_type=jnp.float32)
    gate_pre = stash_rows[:, 0, :].astype(jnp.float32)
    up_pre = stash_rows[:, 1, :].astype(jnp.float32)
    sigmoid_gate = jax.nn.sigmoid(gate_pre)
    grad_gate = (
        hidden_grad * up_pre * sigmoid_gate * (1.0 + gate_pre * (1.0 - sigmoid_gate))
    ).astype(jnp.bfloat16)
    grad_up = (hidden_grad * gate_pre * sigmoid_gate).astype(jnp.bfloat16)
    return grad_gate, grad_up


def made_backward(hidden, gate_cols, up_cols):
    total = jnp.dot(hidden[0], gate_cols.T, preferred_element_type=jnp.float32)
    total = total + jnp.dot(hidden[1], up_cols.T, preferred_element_type=jnp.float32)
    return total.astype(jnp.bfloat16)


def collect(mine, came, capacity, onward, home):
    summed = mine.astype(jnp.float32) + came.astype(jnp.float32)
    width = 2 * capacity

    def sent(k):
        return summed[(REACH + k) * capacity :][:width].astype(jnp.bfloat16)

    def kept(k, arrived):
        total = summed[k * capacity :][:width] + arrived.astype(jnp.float32)
        return total.astype(jnp.bfloat16)

    def homeward(pieces, k):
        return [
            lax.ppermute(pieces[i * capacity :][:capacity], ("section", "expert"), home(k + i, onward))
            for i in (1, 0)
        ][::-1]

    return sent, kept, homeward


def combine(placed, back, gate_values):
    picked = lax.dot_general(
        placed, back, (((0,), (0,)), ((), ())), preferred_element_type=jnp.float32
    )
    return picked * gate_values


def local(
    layer_input,
    cotangent,
    gate_weight,
    up_weight,
    down_weight,
    stashed_pre,
    first_ids,
    first_gates,
    second_ids,
    second_gates,
    keep_mask,
):
    devices = lax.axis_size("expert")
    sections = lax.axis_size("section")
    chips = devices // 2
    pairs = chips // 2
    capacity = stashed_pre.shape[2]
    slots = pairs * capacity
    hidden_local = gate_weight.shape[2]
    out, home, across, beside = routes(devices, sections)
    me = lax.axis_index("expert")
    chip, core = me // 2, me % 2
    ahead = [(i, (i + 1) % sections) for i in range(sections)]
    behind = [((i + 1) % sections, i) for i in range(sections)]
    first_pieces, first_told = prepare(
        False, chip, pairs, capacity, first_ids[..., 0], first_gates[..., 0], keep_mask, layer_input[0]
    )
    second_pieces, second_told = prepare(
        True, chip, pairs, capacity, second_ids[..., 0], second_gates[..., 0], keep_mask, cotangent[0]
    )
    first_near, second_near = first_pieces[1:], second_pieces[1:]
    origins = [
        [(here + jnp.where(here % 2 == 0, -step, step)) % chips for step in range(REACH)]
        for here in (chip, chip ^ 1)
    ]
    origins = origins[0] + origins[1]
    stash_halves = [
        jnp.concatenate(
            [
                lax.dynamic_index_in_dim(stashed_pre[0], 2 * origin + which, 0, False)
                for origin in origins
            ]
        )
        for which in (core, 1 - core)
    ]
    gate_cols = gate_weight[0]
    up_cols = up_weight[0]
    down_rows = down_weight[0]

    V = {}

    def gate(name, value):
        for target, source in WAITS:
            if target == name:
                value = after(value, V[source])
        return value

    V["own_d"] = lax.ppermute(first_pieces[0], "expert", across)
    first_near = [
        lax.ppermute(gate(f"jF{k + 1}", piece), "expert", out(k + 1)) for k, piece in enumerate(first_near)
    ]
    V["jF1"], V["jF2"], V["jF3"] = first_near
    V["own_dB"] = lax.ppermute(gate("ownB", second_pieces[0]), "expert", across)
    own_distants = V["own_d"], V["own_dB"]
    second_near = [gate(f"jB{k + 1}", gate("jB", piece)) for k, piece in enumerate(second_near)]
    second_near = [
        lax.ppermute(piece, "expert", out(k + 1)) for k, piece in enumerate(second_near)
    ]
    V["jB1"], V["jB2"], V["jB3"] = second_near
    first_close = gate("fwdF", jnp.concatenate(first_near))
    first_distant = lax.ppermute(first_close, "expert", across)
    V["fwdF"] = first_distant

    bundles = [
        jnp.concatenate((rows[0], told))
        for rows, told in ((layer_input, first_told), (cotangent, second_told))
    ]

    def relay(first, second):
        V["rF"] = first = lax.ppermute(gate("relayF", first), "section", ahead)
        V["rB"] = second = lax.ppermute(gate("relayB", second), "section", behind)
        return first, second

    V["closeB"] = second_close = gate("fwdB", jnp.concatenate(second_near))
    second_distant = lax.ppermute(second_close, "expert", across)
    V["fwdB"] = second_distant
    told = relay(*bundles)
    held_first = jnp.concatenate(
        [first_pieces[0], *first_near, own_distants[0], first_distant]
    )
    V["heldF"] = held_first = gate("heldF", held_first)
    beside_first = lax.ppermute(held_first, "expert", beside)
    V["coreF"] = beside_first
    first_mine = hidden_forward(gate("hmF", held_first), gate_cols, up_cols)
    V["hmF"] = first_mine[0]
    first_given = hidden_forward(gate("hgF", beside_first), gate_cols, up_cols)
    V["hgF"] = first_given[0]
    first_mine, first_given = lax.optimization_barrier((first_mine, first_given))
    given_first = made_forward((gate("gF", first_given[0]),), down_rows)
    V["gF"] = given_first
    came_first = lax.ppermute(given_first, "expert", beside)
    V["cF"] = came_first
    made_first = lax.optimization_barrier(made_forward((gate("mF", first_mine[0]),), down_rows))
    V["mF"] = made_first

    sent, kept, homeward = collect(made_first, came_first, capacity, 1, home)
    V["payF"] = far = gate("farF", sent(2))
    second_distant = gate("distB", second_distant)
    held_second = jnp.concatenate(
        [second_pieces[0], *second_near, own_distants[1], second_distant]
    )
    V["heldB"] = held_second = gate("heldB", held_second)
    beside_second = lax.ppermute(held_second, "expert", beside)
    V["coreB"] = beside_second
    second_mine = hidden_backward(gate("hmB", held_second), stash_halves[0], down_rows)
    V["hmB"] = second_mine[0]
    second_given = hidden_backward(gate("hgB", beside_second), stash_halves[1], down_rows)
    second_mine, second_given = lax.optimization_barrier((second_mine, second_given))
    given_second = made_backward(second_given, gate_cols, up_cols)
    V["gB"] = given_second
    came_second = lax.ppermute(given_second, "expert", beside)
    V["cB"] = came_second
    second_mine = (gate("mB", second_mine[0]), second_mine[1])
    made_second = lax.optimization_barrier(made_backward(second_mine, gate_cols, up_cols))

    sent2, kept2, homeward2 = collect(made_second, came_second, capacity, -1, home)
    far = lax.ppermute(far, "expert", across)
    V["farF"] = far
    V["payB"] = far2 = gate("farB", sent2(2))
    short = lax.ppermute(gate("shortF", sent(0)), "expert", across)
    V["shortF"] = short
    V["piecesF"] = pieces = gate("homeF", kept(2, far))
    back_first = homeward(pieces, 2)
    V["h2F"], V["h3F"] = back_first
    far2 = lax.ppermute(far2, "expert", across)
    V["farB"] = far2
    last = gate("home0F", kept(0, after(short, pieces)))
    back_first = homeward(last, 0) + back_first
    V["h0F"], V["h1F"] = back_first[:2]
    short2 = lax.ppermute(gate("shortB", sent2(0)), "expert", across)
    pieces = gate("homeB", kept2(2, far2))
    back_second = homeward2(pieces, 2)
    V["h2B"], V["h3B"] = back_second
    pieces = gate("home0B", kept2(0, after(short2, pieces)))
    back_second = homeward2(pieces, 0) + back_second
    count = layer_input.shape[1]

    def unpack(bundle, back):
        lines = bundle[count:, :count].astype(jnp.float32)
        gates = (lines[1] + lines[2]) + lines[3]
        rows = jnp.concatenate(back)
        branch = combine(placement(lines[0].astype(jnp.int32), slots), rows, gates[:, None])
        return branch, bundle[:count].astype(jnp.float32), lines[4][:, None]

    first_branch, tokens, _ = unpack(told[0], back_first)
    second_branch, grads, keep = unpack(told[1], back_second)
    mixed_out = (tokens + first_branch).astype(jnp.bfloat16)
    grad_out = (keep * (grads + second_branch)).astype(jnp.bfloat16)
    return (mixed_out[None], grad_out[None])


def solution(mesh):
    placed = (
        P("section", "expert", None),
        P("section", "expert", None),
        P("section", None, "expert"),
        P("section", None, "expert"),
        P("section", "expert", None),
        P("section", None, None, None, "expert"),
        P("section", "expert", None),
        P("section", "expert", None),
        P("section", "expert", None),
        P("section", "expert", None),
        P("section", "expert"),
    )
    return jax.shard_map(
        local,
        mesh=mesh,
        in_specs=placed,
        out_specs=(P("section", "expert", None), P("section", "expert", None)),
        check_vma=False,
    )
```

```python
import functools

import jax
import jax.numpy as jnp
from jax import lax
from jax.experimental import pallas as pl
from jax.experimental.pallas import tpu as pltpu
from jax.sharding import PartitionSpec as P

REACH = 4
WAITS = (
    ("jB3", "own_d"),
    ("fwdF", "jB1"),
    ("relayB", "own_dB"),
    ("relayF", "own_dB"),
    ("heldB", "rB"),
    ("heldB", "rF"),
    ("heldF", "closeB"),
    ("mF", "gF"),
    ("distB", "gF"),
    ("homeF", "payB"),
    ("shortB", "h3F"),
    ("homeB", "h2F"),
    ("homeB", "h3F"),
    ("home0B", "h0F"),
    ("home0B", "h1F"),
    ("home0F", "payB"),
)


def routes(devices, sections):
    chips = devices // 2

    def nearer(step):
        for chip in range(chips):
            origin = (chip + (step if chip % 2 else -step)) % chips
            for core in range(2):
                yield 2 * origin + core, 2 * chip + core

    def out(step):
        return list(nearer(step))

    def home(step, onward):
        return [
            (s * devices + there, (s + onward) % sections * devices + origin)
            for s in range(sections)
            for origin, there in nearer(step)
        ]

    across = [(i, i ^ 2) for i in range(devices)]
    beside = [(i, i ^ 1) for i in range(devices)]
    return out, home, across, beside


def prepare_kernel(pairs, capacity, masked, chip_ref, ids_ref, gates_ref, keep_ref, rows_ref, *outs):
    count, rows = ids_ref.shape[1], rows_ref[...]
    chip = chip_ref[0]
    kept = keep_ref[...].astype(jnp.float32)
    before = lax.broadcasted_iota(jnp.int32, (count, count), 0)
    before = (before < lax.broadcasted_iota(jnp.int32, (count, count), 1)).astype(jnp.bfloat16)
    ahead = ids_ref[...] - lax.div(chip, 2)
    ahead = jnp.where(ahead < 0, ahead + pairs, ahead)
    near = jnp.where(lax.rem(chip, 2) == 1, 1, pairs - 1)
    step = jnp.where(ahead == 0, 0, jnp.where(ahead == 2, 3, jnp.where(ahead == near, 1, 2)))
    chosen = jnp.where(lax.broadcasted_iota(jnp.int32, (8, count), 0) == step, 1.0, 0.0)
    earlier = jnp.dot(chosen.astype(jnp.bfloat16), before, preferred_element_type=jnp.float32)
    slot = jnp.sum(chosen * earlier, axis=0, keepdims=True).astype(jnp.int32)
    place = step * capacity + slot
    here = lax.broadcasted_iota(jnp.int32, (REACH * capacity, count), 0) == place
    here = jnp.where(here, kept if masked else 1.0, 0.0).astype(jnp.bfloat16)
    made = jnp.dot(here, rows, preferred_element_type=jnp.float32)
    for k in range(REACH):
        outs[k][...] = made[k * capacity : (k + 1) * capacity].astype(jnp.bfloat16)
    gates = gates_ref[...]
    high = gates.astype(jnp.bfloat16).astype(jnp.float32)
    middle = (gates - high).astype(jnp.bfloat16).astype(jnp.float32)
    row = lax.broadcasted_iota(jnp.int32, (8, count), 0)
    lines = jnp.zeros((8, count), jnp.float32)
    for k, line in enumerate((place.astype(jnp.float32), high, middle, gates - high - middle, kept)):
        lines = jnp.where(row == k, line, lines)
    told = outs[REACH]
    told[...] = jnp.zeros_like(told)
    told[:, 0:count] = lines.astype(told.dtype)


def prepare(masked, chip, pairs, capacity, ids, gates, keep, rows):
    count, width = rows.shape
    whole = pl.BlockSpec(memory_space=pltpu.VMEM)
    made = pl.pallas_call(
        functools.partial(prepare_kernel, pairs, capacity, masked),
        out_shape=[jax.ShapeDtypeStruct((capacity, width), jnp.bfloat16)] * REACH
        + [jax.ShapeDtypeStruct((8, width), jnp.bfloat16)],
        in_specs=[pl.BlockSpec(memory_space=pltpu.SMEM)] + [whole] * 4,
        out_specs=[whole] * (REACH + 1),
        cost_estimate=pl.CostEstimate(
            flops=2 * REACH * capacity * count * width,
            bytes_accessed=4 * count * width,
            transcendentals=0,
        ),
        name="prepare_second" if masked else "prepare_first",
    )(chip[None], ids, gates, keep, rows)
    return made[:REACH], made[REACH]


def placement(slot_at, slot_total):
    rows = lax.broadcasted_iota(jnp.int32, (slot_total, slot_at.shape[0]), 0)
    return (rows == slot_at[None, :]).astype(jnp.bfloat16)


def after(value, *others):
    return lax.optimization_barrier((value, *others))[0]


def hidden_forward(routed, gate_cols, up_cols):
    gate_pre = jnp.dot(routed, gate_cols, preferred_element_type=jnp.float32)
    up_pre = jnp.dot(routed, up_cols, preferred_element_type=jnp.float32)
    return ((jax.nn.silu(gate_pre) * up_pre).astype(jnp.bfloat16),)


def made_forward(hidden, down_rows):
    return jnp.dot(hidden[0], down_rows, preferred_element_type=jnp.float32).astype(jnp.bfloat16)


def hidden_backward(routed, stash_rows, down_rows):
    hidden_grad = jnp.dot(routed, down_rows.T, preferred_element_type=jnp.float32)
    gate_pre = stash_rows[:, 0, :].astype(jnp.float32)
    up_pre = stash_rows[:, 1, :].astype(jnp.float32)
    sigmoid_gate = jax.nn.sigmoid(gate_pre)
    grad_gate = (
        hidden_grad * up_pre * sigmoid_gate * (1.0 + gate_pre * (1.0 - sigmoid_gate))
    ).astype(jnp.bfloat16)
    grad_up = (hidden_grad * gate_pre * sigmoid_gate).astype(jnp.bfloat16)
    return grad_gate, grad_up


def made_backward(hidden, gate_cols, up_cols):
    total = jnp.dot(hidden[0], gate_cols.T, preferred_element_type=jnp.float32)
    total = total + jnp.dot(hidden[1], up_cols.T, preferred_element_type=jnp.float32)
    return total.astype(jnp.bfloat16)


def collect(mine, came, capacity, onward, home):
    summed = mine.astype(jnp.float32) + came.astype(jnp.float32)
    width = 2 * capacity

    def sent(k):
        return summed[(REACH + k) * capacity :][:width].astype(jnp.bfloat16)

    def kept(k, arrived):
        total = summed[k * capacity :][:width] + arrived.astype(jnp.float32)
        return total.astype(jnp.bfloat16)

    def homeward(pieces, k):
        return [
            lax.ppermute(pieces[i * capacity :][:capacity], ("section", "expert"), home(k + i, onward))
            for i in (1, 0)
        ][::-1]

    return sent, kept, homeward


def combine(placed, back, gate_values):
    picked = lax.dot_general(
        placed, back, (((0,), (0,)), ((), ())), preferred_element_type=jnp.float32
    )
    return picked * gate_values


def local(
    layer_input,
    cotangent,
    gate_weight,
    up_weight,
    down_weight,
    stashed_pre,
    first_ids,
    first_gates,
    second_ids,
    second_gates,
    keep_mask,
):
    devices = lax.axis_size("expert")
    sections = lax.axis_size("section")
    chips = devices // 2
    pairs = chips // 2
    capacity = stashed_pre.shape[2]
    slots = pairs * capacity
    hidden_local = gate_weight.shape[2]
    out, home, across, beside = routes(devices, sections)
    me = lax.axis_index("expert")
    chip, core = me // 2, me % 2
    ahead = [(i, (i + 1) % sections) for i in range(sections)]
    behind = [((i + 1) % sections, i) for i in range(sections)]
    first_pieces, first_told = prepare(
        False, chip, pairs, capacity, first_ids[..., 0], first_gates[..., 0], keep_mask, layer_input[0]
    )
    second_pieces, second_told = prepare(
        True, chip, pairs, capacity, second_ids[..., 0], second_gates[..., 0], keep_mask, cotangent[0]
    )
    first_near, second_near = first_pieces[1:], second_pieces[1:]
    origins = [
        [(here + jnp.where(here % 2 == 0, -step, step)) % chips for step in range(REACH)]
        for here in (chip, chip ^ 1)
    ]
    origins = origins[0] + origins[1]
    stash_halves = [
        jnp.concatenate(
            [
                lax.dynamic_index_in_dim(stashed_pre[0], 2 * origin + which, 0, False)
                for origin in origins
            ]
        )
        for which in (core, 1 - core)
    ]
    gate_cols = gate_weight[0]
    up_cols = up_weight[0]
    down_rows = down_weight[0]

    V = {}

    def gate(name, value):
        for target, source in WAITS:
            if target == name:
                value = after(value, V[source])
        return value

    V["own_d"] = lax.ppermute(first_pieces[0], "expert", across)
    first_near = [
        lax.ppermute(gate(f"jF{k + 1}", piece), "expert", out(k + 1)) for k, piece in enumerate(first_near)
    ]
    V["jF1"], V["jF2"], V["jF3"] = first_near
    V["own_dB"] = lax.ppermute(gate("ownB", second_pieces[0]), "expert", across)
    own_distants = V["own_d"], V["own_dB"]
    second_near = [gate(f"jB{k + 1}", gate("jB", piece)) for k, piece in enumerate(second_near)]
    second_near = [
        lax.ppermute(piece, "expert", out(k + 1)) for k, piece in enumerate(second_near)
    ]
    V["jB1"], V["jB2"], V["jB3"] = second_near
    first_close = gate("fwdF", jnp.concatenate(first_near))
    first_distant = lax.ppermute(first_close, "expert", across)
    V["fwdF"] = first_distant

    bundles = [
        jnp.concatenate((rows[0], told))
        for rows, told in ((layer_input, first_told), (cotangent, second_told))
    ]

    def relay(first, second):
        V["rF"] = first = lax.ppermute(gate("relayF", first), "section", ahead)
        V["rB"] = second = lax.ppermute(gate("relayB", second), "section", behind)
        return first, second

    V["closeB"] = second_close = gate("fwdB", jnp.concatenate(second_near))
    second_distant = lax.ppermute(second_close, "expert", across)
    V["fwdB"] = second_distant
    told = relay(*bundles)
    held_first = jnp.concatenate(
        [first_pieces[0], *first_near, own_distants[0], first_distant]
    )
    V["heldF"] = held_first = gate("heldF", held_first)
    beside_first = lax.ppermute(held_first, "expert", beside)
    V["coreF"] = beside_first
    first_mine = hidden_forward(gate("hmF", held_first), gate_cols, up_cols)
    V["hmF"] = first_mine[0]
    first_given = hidden_forward(gate("hgF", beside_first), gate_cols, up_cols)
    V["hgF"] = first_given[0]
    first_mine, first_given = lax.optimization_barrier((first_mine, first_given))
    given_first = made_forward((gate("gF", first_given[0]),), down_rows)
    V["gF"] = given_first
    came_first = lax.ppermute(given_first, "expert", beside)
    V["cF"] = came_first
    made_first = lax.optimization_barrier(made_forward((gate("mF", first_mine[0]),), down_rows))
    V["mF"] = made_first

    sent, kept, homeward = collect(made_first, came_first, capacity, 1, home)
    V["payF"] = far = gate("farF", sent(2))
    second_distant = gate("distB", second_distant)
    held_second = jnp.concatenate(
        [second_pieces[0], *second_near, own_distants[1], second_distant]
    )
    V["heldB"] = held_second = gate("heldB", held_second)
    beside_second = lax.ppermute(held_second, "expert", beside)
    V["coreB"] = beside_second
    second_mine = hidden_backward(gate("hmB", held_second), stash_halves[0], down_rows)
    V["hmB"] = second_mine[0]
    second_given = hidden_backward(gate("hgB", beside_second), stash_halves[1], down_rows)
    second_mine, second_given = lax.optimization_barrier((second_mine, second_given))
    given_second = made_backward(second_given, gate_cols, up_cols)
    V["gB"] = given_second
    came_second = lax.ppermute(given_second, "expert", beside)
    V["cB"] = came_second
    second_mine = (gate("mB", second_mine[0]), second_mine[1])
    made_second = lax.optimization_barrier(made_backward(second_mine, gate_cols, up_cols))

    sent2, kept2, homeward2 = collect(made_second, came_second, capacity, -1, home)
    far = lax.ppermute(far, "expert", across)
    V["farF"] = far
    V["payB"] = far2 = gate("farB", sent2(2))
    short = lax.ppermute(gate("shortF", sent(0)), "expert", across)
    V["shortF"] = short
    V["piecesF"] = pieces = gate("homeF", kept(2, far))
    back_first = homeward(pieces, 2)
    V["h2F"], V["h3F"] = back_first
    far2 = lax.ppermute(far2, "expert", across)
    V["farB"] = far2
    last = gate("home0F", kept(0, after(short, pieces)))
    back_first = homeward(last, 0) + back_first
    V["h0F"], V["h1F"] = back_first[:2]
    short2 = lax.ppermute(gate("shortB", sent2(0)), "expert", across)
    pieces = gate("homeB", kept2(2, far2))
    back_second = homeward2(pieces, 2)
    V["h2B"], V["h3B"] = back_second
    pieces = gate("home0B", kept2(0, after(short2, pieces)))
    back_second = homeward2(pieces, 0) + back_second
    count = layer_input.shape[1]

    def unpack(bundle, back):
        lines = bundle[count:, :count].astype(jnp.float32)
        gates = (lines[1] + lines[2]) + lines[3]
        rows = jnp.concatenate(back)
        branch = combine(placement(lines[0].astype(jnp.int32), slots), rows, gates[:, None])
        return branch, bundle[:count].astype(jnp.float32), lines[4][:, None]

    first_branch, tokens, _ = unpack(told[0], back_first)
    second_branch, grads, keep = unpack(told[1], back_second)
    mixed_out = (tokens + first_branch).astype(jnp.bfloat16)
    grad_out = (keep * (grads + second_branch)).astype(jnp.bfloat16)
    return (mixed_out[None], grad_out[None])


def solution(mesh):
    placed = (
        P("section", "expert", None),
        P("section", "expert", None),
        P("section", None, "expert"),
        P("section", None, "expert"),
        P("section", "expert", None),
        P("section", None, None, None, "expert"),
        P("section", "expert", None),
        P("section", "expert", None),
        P("section", "expert", None),
        P("section", "expert", None),
        P("section", "expert"),
    )
    return jax.shard_map(
        local,
        mesh=mesh,
        in_specs=placed,
        out_specs=(P("section", "expert", None), P("section", "expert", None)),
        check_vma=False,
    )
```
